128 devices in a mesh: cent: 16 (over z, y), grp: 8 (over x, core).
Axes of the slice: x: 4, y: 4, z: 4, core: 2. Of those that a mesh axis runs over, the one named last changes fastest.
Arguments:
- queries: bfloat16 [256, 32, 128], P('grp'), may hold values from -6 to 6
- centroids: bfloat16 [524288, 128], P('cent'), may hold values from -0.5 to 0.5
- candidates: int32 [8, 16, 2, 64], P('grp', 'cent'), may hold values from 0 to 65535, as said below
- token_codes: int32 [65536, 128], P(('cent', 'grp')), may hold values from 0 to 32767
- resid_words: int32 [65536, 32, 128], P(('cent', 'grp')), may hold values from 0 to 255
- lengths: int32 [65536], P(('cent', 'grp')), may hold values from 1 to 128
- levels: float32 [4, 128], replicated, may hold values from -0.3125 to 0.3125
Outputs:
- token_best: float32 [256, 32], P('grp')
- passage_scores: float32 [8, 16, 2, 64], P('grp', 'cent')
The draws below stay inside these ranges and needn't reach their ends.
Inputs may be any that keep to these rules, and one draw needn't show every extreme that they name: `candidates`: the entries of one [g, c] block are all different and name at most 2 passages of any one owner block (passages owner * 512 to owner * 512 + 511); one owner block gets exactly 2 from every [g, c] block.
All inputs are finite; a program needn't handle non-finite values.
Results may differ from the reference program's by a relative error of at most 0.0003.
Values may be sent and summed in bfloat16 or wider, within the bound.
A program may use at most 128 MiB of HBM per device.

```python
import jax
import jax.numpy as jnp
from jax import lax

D = 128
QT = 32
CENT_DEV = 32768
PLEN = 128
NCAND = 64
QRY_DEV = 2
PASS_DEV = 512
GROUPS = 8
CSH = 16
NQ = 256
NCENT = 524288
NPASS = 65536
PACKED = 32
CAP = 2


def draw_candidates(key, part):
    base_key = jax.random.fold_in(key, 11)
    pair_count = QRY_DEV * NCAND
    owner_total = GROUPS * CSH
    token_total = owner_total * CAP
    hot_key, tier_key, block_key = jax.random.split(base_key, 3)
    popular_holder = jax.random.randint(hot_key, (), 0, owner_total)
    holder_levels = jax.random.randint(tier_key, (owner_total,), 0, 4)

    def one_block(source):
        source_key = jax.random.fold_in(block_key, source)
        noise_key, order_key, offset_key = jax.random.split(source_key, 3)
        token_numbers = jnp.arange(token_total, dtype=jnp.int32)
        token_holder = token_numbers // CAP
        random_jitter = jax.random.randint(noise_key, (token_total,), 0, 65536)
        extra_credit = jnp.where(token_holder == popular_holder, 262144, jnp.take(holder_levels, token_holder) * 16384)
        rank_weight = (random_jitter + extra_credit) * 4096 + token_numbers
        top_values, chosen = lax.top_k(rank_weight, pair_count)
        chosen = jax.random.permutation(order_key, chosen)
        chosen_owner = chosen // CAP
        chosen_slot = chosen % CAP
        offsets = jax.random.randint(offset_key, (owner_total,), 0, PASS_DEV)
        local_ids = (jnp.take(offsets, chosen_owner) + chosen_slot) % PASS_DEV
        return (chosen_owner * PASS_DEV + local_ids).astype(jnp.int32)
    blocks = jax.vmap(one_block)(jnp.arange(owner_total, dtype=jnp.int32))
    blocks = blocks.reshape(CSH, GROUPS, QRY_DEV, NCAND)
    return jnp.transpose(blocks, (1, 0, 2, 3))


def draw_lengths(key, part):
    base_key = jax.random.fold_in(key, 23)
    values = jax.random.randint(base_key, (NPASS,), 1, PLEN + 1)
    return values.at[0].set(PLEN).at[1].set(1).astype(jnp.int32)


def touch_ends(entries, stream_key, low, high):
    dims = entries.shape
    index_at = [jax.random.randint(jax.random.fold_in(stream_key, axis), (), 0, dims[axis]) for axis in range(len(dims))]
    entries = entries.at[tuple(index_at)].set(low)
    longest = dims.index(max(dims))
    index_at[longest] = (index_at[longest] + 1) % dims[longest]
    return entries.at[tuple(index_at)].set(high)


def block_levels(rng, shape, cuts, smallest, largest):
    factor_of = 1.0
    for dim, shards_of in cuts:
        draws = jax.random.uniform(jax.random.fold_in(jax.random.fold_in(rng, 6), dim), (shards_of,), jnp.float32, smallest / len(cuts), largest / len(cuts))
        factor_of = factor_of * jnp.repeat(jnp.exp(draws), shape[dim] // shards_of).reshape((-1,) + (1,) * (len(shape) - 1 - dim))
    return factor_of


def gaussian(stream_key, extent, spread, reach, cuts=(), kind=jnp.bfloat16):
    factor_of = block_levels(stream_key, extent, cuts, -0.22, 0.18) if cuts else 1.0
    values = jax.random.normal(stream_key, extent, jnp.float32) * spread * factor_of
    return jnp.minimum(jnp.maximum(values, -reach), reach).astype(kind)


def setup_inputs(seed: int = 0) -> dict:
    key_of = jax.random.split(jax.random.key(seed), 8)
    queries = gaussian(key_of[0], (NQ, QT, D), 1.0, 6.0, ((0, 8),))
    centroids = gaussian(key_of[1], (NCENT, D), D ** -0.5, 0.5, ((0, 16),))
    candidates = draw_candidates(jax.random.fold_in(key_of[7], 71), 0)
    token_codes = touch_ends(jax.random.randint(key_of[3], (NPASS, PLEN), 0, CENT_DEV), jax.random.fold_in(key_of[3], 1), 0, CENT_DEV - 1).astype(jnp.int32)
    resid_words = touch_ends(jax.random.randint(key_of[4], (NPASS, PACKED, D), 0, 256), jax.random.fold_in(key_of[4], 1), 0, 255).astype(jnp.int32)
    lengths = draw_lengths(jax.random.fold_in(key_of[7], 71), 0)
    levels = gaussian(key_of[6], (4, D), 0.05, 0.3125, (), jnp.float32)
    return dict(queries=queries, centroids=centroids, candidates=candidates, token_codes=token_codes, resid_words=resid_words, lengths=lengths, levels=levels)


def unpack_levels(words, levels):
    fields = []
    for shift_index in range(4):
        fields.append(jnp.bitwise_and(jnp.right_shift(words, 2 * shift_index), 3))
    stacked = jnp.stack(fields, axis=2)
    level_codes = stacked.reshape(words.shape[0], words.shape[1] * 4, words.shape[2])
    result = jnp.zeros(level_codes.shape, jnp.float32)
    for level_index in range(4):
        result = result + jnp.where(level_codes == level_index, levels[level_index], 0.0)
    return result

def dequantize(centroid_rows, words, levels):
    dequantized = centroid_rows.astype(jnp.float32) + unpack_levels(words, levels)
    inverse_norm = lax.rsqrt(lax.optimization_barrier(jnp.sum(dequantized * dequantized, axis=-1, keepdims=True)) + 1e-06)
    return (dequantized * inverse_norm).astype(jnp.bfloat16)

def reference(queries, centroids, candidates, token_codes, resid_words, lengths, levels):
    query_count = queries.shape[0]
    flat_queries = queries.reshape(query_count * QT, D).astype(jnp.float32)
    wide_table = centroids.astype(jnp.float32)
    block_size = min(CENT_DEV, 2048)
    block_total = centroids.shape[0] // block_size

    def block_step(block_index, running_best):
        start = (block_index * block_size).astype(jnp.int32)
        centroid_block = lax.dynamic_slice_in_dim(wide_table, start, block_size, 0)
        scores = jnp.dot(flat_queries, centroid_block.T, preferred_element_type=jnp.float32)
        return jnp.maximum(running_best, lax.optimization_barrier(jnp.max(scores, axis=1)))
    initial = jnp.full((query_count * QT,), -jnp.inf, jnp.float32)
    token_best = lax.fori_loop(0, block_total, block_step, initial).reshape(query_count, QT)
    cand_rows = candidates.reshape(query_count, NCAND)

    def one_query(inputs):
        query_tokens, cand_ids = inputs
        owners = cand_ids // PASS_DEV
        shard_index = owners // GROUPS
        global_codes = (jnp.take(token_codes, cand_ids, axis=0) + (shard_index * CENT_DEV)[:, None]).astype(jnp.int32)
        centroid_rows = jnp.take(centroids, global_codes, axis=0)
        embedded = dequantize(centroid_rows, jnp.take(resid_words, cand_ids, axis=0), levels)
        scores = jnp.einsum('qd,spd->sqp', query_tokens.astype(jnp.float32), embedded.astype(jnp.float32))
        position = lax.broadcasted_iota(jnp.int32, scores.shape, 2)
        inside = position < jnp.take(lengths, cand_ids)[:, None, None]
        maxima = lax.optimization_barrier(jnp.max(jnp.where(inside, scores, -1000000000.0), axis=2))
        return lax.optimization_barrier(jnp.sum(maxima, axis=1)) / QT
    passage_scores = lax.map(one_query, (queries, cand_rows))
    return (token_best, passage_scores.reshape(GROUPS, CSH, QRY_DEV, NCAND))
```

```python
import functools

import jax
import jax.numpy as jnp
from jax import lax
from jax.experimental import pallas as pl
from jax.experimental.pallas import tpu as pltpu
from jax.sharding import PartitionSpec as P

MESH = pl.DeviceIdType.MESH
ANY = pl.BlockSpec(memory_space=pl.ANY)
VMEM = pl.BlockSpec(memory_space=pltpu.VMEM)
SMEM = pl.BlockSpec(memory_space=pltpu.SMEM)
EMPTY = 1 << 20
MASKED = -1000000000.0
UNITS = 8
BATCH = 16
PIECE = 1024
OPENING = 16


def greet(axis_peers):
    barrier = pltpu.get_barrier_semaphore()
    total = 0
    for axis, me, size in axis_peers:
        for d in range(1, size):
            pl.semaphore_signal(
                barrier, inc=1, device_id={axis: lax.rem(me + d, size)}, device_id_type=MESH
            )
            total += 1
    pl.semaphore_wait(barrier, total)


def push(src, dst, send, recv, axis, peer):
    return pltpu.make_async_remote_copy(
        src_ref=src,
        dst_ref=dst,
        send_sem=send,
        recv_sem=recv,
        device_id={axis: peer},
        device_id_type=MESH,
    )


def search_kernel(
    cents, groups, pass_dev, block, head, cand_count,
    q_ref, cand_ref, codes_ref, cent_hbm, words_hbm,
    table_ref, tail_ref, words_ref, qall_ref, qt_ref, acc_ref, picks_ref, ends_ref, entry_ref,
    head_buf, row_buf, all_buf, rows, csem, wsem, own_sem, s1, r1, s2, r2, sq, rq,
):
    me_c, me_g = lax.axis_index("cent"), lax.axis_index("grp")
    partner = me_g + 1 - 2 * lax.rem(me_g, 2)
    ahead, behind = lax.rem(me_g + 2, groups), lax.rem(me_g + groups - 2, groups)
    across = lax.rem(me_g + 4, groups)
    steps = head // block
    tiles, width = qt_ref.shape[0], qt_ref.shape[2]
    half = q_ref.shape[0] // 2

    def fetch(b):
        src = cent_hbm.at[pl.ds(pl.multiple_of(b * block, block), block)]
        return pltpu.make_async_copy(
            src, head_buf.at[pl.ds(pl.multiple_of(b * block, block), block)], csem.at[0, b]
        )

    def fetch_tail(b):
        src = cent_hbm.at[pl.ds(pl.multiple_of(head + b * block, block), block)]
        return pltpu.make_async_copy(
            src, tail_ref.at[pl.ds(pl.multiple_of(b * block, block), block)], csem.at[1, b]
        )

    for b in range(steps):
        fetch(b).start()
        fetch_tail(b).start()
    words_copy = pltpu.make_async_copy(words_hbm, words_ref, wsem)
    words_copy.start()
    own = pltpu.make_async_copy(q_ref, qall_ref.at[me_g], own_sem)
    own.start()
    row_buf[me_c] = jnp.concatenate([cand_ref[0:1, :], cand_ref[1:2, :]], axis=1)
    for t in range(tiles):
        qt_ref[t] = q_ref[t * width : (t + 1) * width, :].T
    acc_ref[...] = jnp.full(acc_ref.shape, -jnp.inf, jnp.float32)
    by_token = codes_ref[...].T
    for part in range(codes_ref.shape[1] // 32):
        span = slice(part * pass_dev, (part + 1) * pass_dev)
        picks_ref[:, span] = by_token[part * 32 : (part + 1) * 32, :]
    greet((("cent", me_c, cents), ("grp", me_g, groups)))

    gather_rows = [
        push(row_buf.at[me_c], row_buf.at[me_c], s1.at[d], r1.at[d], "cent", lax.rem(me_c + d, cents))
        for d in range(1, cents)
    ]
    gather_groups = [
        push(row_buf, all_buf.at[me_g], s2.at[d], r2.at[d], "grp", lax.rem(me_g + d, groups))
        for d in range(1, groups)
    ]

    def hand(k, block_of, peer, start=0, size=2 * half):
        held = qall_ref.at[block_of, pl.ds(start, size)]
        return push(held, held, sq.at[k], rq.at[k], "grp", peer)

    to_ahead = push(q_ref, qall_ref.at[me_g], sq.at[0], rq.at[0], "grp", ahead)
    to_behind = push(q_ref, qall_ref.at[me_g], sq.at[1], rq.at[1], "grp", behind)
    to_partner = push(q_ref, qall_ref.at[me_g], sq.at[2], rq.at[2], "grp", partner)
    relay_ahead = hand(3, behind, ahead, 0, half)
    relay_behind = hand(4, ahead, behind, half, half)
    share_behind = hand(5, behind, partner)
    share_ahead = hand(6, ahead, partner)
    share_low = hand(7, across, partner, 0, half)
    share_high = hand(8, across, partner, half, half)

    for copy in gather_rows:
        copy.start()
    to_ahead.start()
    to_behind.start()
    to_partner.start()

    def step(b, _):
        fetch(b).wait()
        fetch_tail(b).wait()

        @pl.when(b == min(2, steps - 1))
        def _():
            for copy in gather_rows:
                copy.wait_recv()
            for copy in gather_groups:
                copy.start()

        @pl.when(b == min(3, steps - 1))
        def _():
            to_ahead.wait_recv()
            relay_ahead.start()
            share_behind.start()
            to_behind.wait_recv()
            relay_behind.start()
            share_ahead.start()

        here = pl.ds(pl.multiple_of(b * block, block), block)
        there = pl.ds(pl.multiple_of(head + b * block, block), block)
        table_ref[here, :] = head_buf[here, :].astype(jnp.float32)
        table_ref[there, :] = tail_ref[here, :].astype(jnp.float32)
        for t in range(tiles):
            scores = jnp.dot(head_buf[here, :], qt_ref[t], preferred_element_type=jnp.float32)
            top = jnp.max(scores.reshape(block // 8, 8, width), axis=0)
            acc_ref[t] = jnp.maximum(acc_ref[t], top)
        return 0

    lax.fori_loop(0, steps, step, 0)

    relay_ahead.wait_recv()
    share_low.start()
    relay_behind.wait_recv()
    share_high.start()
    for copy in gather_groups:
        copy.wait_recv()
    all_buf[me_g] = row_buf[...]
    for g in range(groups):
        for c in range(cents):
            rows[pl.ds(g * cents + c, 1), :] = all_buf[g, c]
    found = rows[...]
    lane = lax.broadcasted_iota(jnp.int32, found.shape, 1)
    mine = jnp.right_shift(found, pass_dev.bit_length() - 1) == me_c * groups + me_g
    packed = (lane * pass_dev + jnp.bitwise_and(found, pass_dev - 1)).astype(jnp.float32)
    first = jnp.min(jnp.where(mine, packed, float(EMPTY)), axis=1, keepdims=True)
    last = jnp.max(jnp.where(mine, packed, -1.0), axis=1, keepdims=True)
    ends = jnp.where(lane == 0, first, jnp.where(lane == 1, last, 0.0))
    ends_ref[...] = ends
    turned = ends.T[0:8, :].astype(jnp.int32)
    source = lax.broadcasted_iota(jnp.int32, turned.shape, 1)
    slot = lax.broadcasted_iota(jnp.int32, turned.shape, 0)
    other = jnp.where(slot == 1, jnp.broadcast_to(turned[0:1, :], turned.shape), -1)
    there = (turned < EMPTY) & (turned > other)
    query = 2 * source + jnp.right_shift(turned, (pass_dev * cand_count).bit_length() - 1)
    entry = jnp.bitwise_and(turned, pass_dev - 1) + pass_dev * (
        query + 2 * cents * groups * (slot * cents * groups + source)
    )
    entry_ref[...] = jnp.where(there, entry, -1)

    own.wait()
    words_copy.wait()
    for copy in gather_rows + gather_groups:
        copy.wait_send()
    for copy in (to_ahead, to_behind, relay_ahead, relay_behind):
        copy.wait_send()
    for copy in (to_partner, share_behind, share_ahead, share_low, share_high):
        copy.wait()


def passage_kernel(
    cents, groups, pass_dev, plen, qtok, opening,
    entries, len_ref, ends_ref, lev_ref, picks_ref, table, tail, words, q_ref, qt_ref, acc_in,
    out_ref, best_ref,
    items, embeds, totals, acc, csem, *picks,
):
    srcs = groups * cents
    tiles = qt_ref.shape[0]
    rows_of_piece = PIECE
    pieces = tail.shape[0] // rows_of_piece * tiles
    loads = [
        pltpu.make_async_copy(picks_ref.at[r], picks[r], csem.at[r]) for r in range(len(picks))
    ]
    for copy in loads:
        copy.start()
    acc[...] = acc_in[...]

    def piece(m):
        t = lax.rem(m, tiles)
        start = pl.multiple_of(m // tiles * rows_of_piece, rows_of_piece)
        scores = jnp.dot(
            tail[pl.ds(start, rows_of_piece), :], qt_ref[t], preferred_element_type=jnp.float32
        )
        top = jnp.max(scores.reshape(rows_of_piece // 8, 8, scores.shape[1]), axis=0)
        acc[t] = jnp.maximum(acc[t], top)

    def collect(src, count):
        for slot in range(2):
            entry = entries[slot, src]
            items[count] = entry
            count = count + jnp.where(entry >= 0, 1, 0)
        return count

    def open_step(m, count):
        piece(m)
        for k in range(srcs // opening):
            count = collect(m * (srcs // opening) + k, count)
        return count

    count = lax.fori_loop(0, opening, open_step, jnp.int32(0))
    for pad in range(BATCH):
        items[count + pad] = 2 * srcs * (2 * srcs) * pass_dev
    totals[...] = jnp.zeros(totals.shape, jnp.float32)
    for copy in loads:
        copy.wait()

    sub = lax.broadcasted_iota(jnp.int32, (8, 128), 0)
    level = [jnp.broadcast_to(lev_ref[k : k + 1, :], (8, 128)) for k in range(4)]

    def embed(passage, part):
        word = words[passage, pl.ds(pl.multiple_of(part * 8, 8), 8), :]
        at = part * pass_dev + passage
        tiles = []
        for j in range(4):
            rows = None
            for s in range(8):
                row = table[pl.ds(picks[4 * s + j][at], 1), :]
                row = jnp.broadcast_to(row, (8, 128))
                rows = row if rows is None else jnp.where(sub == s, row, rows)
            low = jnp.bitwise_and(word, 1 << (2 * j)) != 0
            high = jnp.bitwise_and(word, 2 << (2 * j)) != 0
            residual = jnp.where(
                high, jnp.where(low, level[3], level[2]), jnp.where(low, level[1], level[0])
            )
            dense = rows + residual
            squares = jnp.sum(dense * dense, axis=1, keepdims=True)
            tiles.append(dense * lax.rsqrt(squares + 1e-06))
        return jnp.concatenate(tiles, axis=0).astype(jnp.bfloat16)

    def embed_units(item, part):
        done = []
        for _ in range(UNITS):
            passage = jnp.bitwise_and(items[item], pass_dev - 1)
            done.append((item, part, embed(passage, part)))
            ends = (part + 1) * 32 >= len_ref[passage]
            inside = item < count
            item, part = (
                jnp.where(inside & ends, item + 1, item),
                jnp.where(inside, jnp.where(ends, 0, part + 1), part),
            )
        for at, block, value in done:
            embeds[at, pl.ds(pl.multiple_of(block * 32, 32), 32), :] = value
        return item, part

    def both_step(state):
        item, part, m = state
        piece(m)
        item, part = embed_units(item, part)
        return item, part, m + 1

    def embed_step(state):
        return embed_units(*state)

    def piece_step(m, _):
        piece(m)
        return 0

    item, part, m = lax.while_loop(
        lambda s: (s[0] < count) & (s[2] < pieces),
        both_step,
        (jnp.int32(0), jnp.int32(0), jnp.int32(opening)),
    )
    lax.while_loop(lambda s: s[0] < count, embed_step, (item, part))
    lax.fori_loop(m, pieces, piece_step, 0)
    for t in range(tiles):
        width = acc.shape[2]
        best_ref[:, t * width : (t + 1) * width] = jnp.max(acc[t], axis=0, keepdims=True)

    sub_q = lax.broadcasted_iota(jnp.int32, (8, qtok), 0)

    def score_step(batch, _):
        for k in range(BATCH):
            i = batch * BATCH + k
            entry = items[i]
            query = jnp.bitwise_and(jnp.right_shift(entry, pass_dev.bit_length() - 1), 2 * srcs - 1)
            row = jnp.right_shift(entry, (2 * srcs * pass_dev).bit_length() - 1)
            length = len_ref[jnp.bitwise_and(entry, pass_dev - 1)]
            scores = lax.dot_general(
                embeds[i], q_ref[query], (((1,), (1,)), ((), ())), preferred_element_type=jnp.float32
            )
            top = None
            for part in range(plen // 32):
                for j in range(4):
                    at = part * 32 + j * 8
                    inside = 4 * sub_q + (part * 32 + j) < length
                    tile = jnp.where(inside, scores[at : at + 8], MASKED)
                    top = tile if top is None else jnp.maximum(top, tile)
            totals[pl.ds(row, 1), 0:qtok] = jnp.max(top, axis=0, keepdims=True)
        return 0

    lax.fori_loop(0, pl.cdiv(count, BATCH), score_step, 0)

    value = jnp.sum(totals[0 : 2 * srcs, :], axis=1, keepdims=True) * (1.0 / qtok)
    ends = ends_ref[...]
    lane = lax.broadcasted_iota(jnp.int32, (srcs, srcs), 1)
    place = jnp.right_shift(ends.astype(jnp.int32), pass_dev.bit_length() - 1)
    low, high = place[:, 0:1], place[:, 1:2]
    second = ends[:, 1:2] > ends[:, 0:1]
    out_ref[...] = jnp.where(lane == low, value[0:srcs], 0.0) + jnp.where(
        (lane == high) & second, value[srcs : 2 * srcs], 0.0
    )


def return_kernel(
    cents, groups,
    best_ref, part_ref,
    token_ref, score_ref,
    best_buf, part_buf, sum_buf, row_buf, sb, rb, s1, r1, s2, r2,
):
    me_c, me_g = lax.axis_index("cent"), lax.axis_index("grp")
    greet((("cent", me_c, cents), ("grp", me_g, groups)))

    def rows_of(g):
        return part_ref.at[pl.ds(pl.multiple_of(g * cents, cents), cents)]

    blocks, tops, lines = [], [], []
    for d in range(1, groups):
        peer = lax.rem(me_g + d, groups)
        blocks.append(push(rows_of(peer), part_buf.at[me_g], s1.at[d], r1.at[d], "grp", peer))
    for d in range(1, cents):
        peer = lax.rem(me_c + d, cents)
        tops.append(push(best_ref, best_buf.at[me_c], sb.at[d], rb.at[d], "cent", peer))
        lines.append(push(sum_buf.at[peer], row_buf.at[me_c], s2.at[d], r2.at[d], "cent", peer))
    for copy in blocks:
        copy.start()
    for copy in tops:
        copy.start()
    part_buf[me_g] = part_ref[pl.ds(pl.multiple_of(me_g * cents, cents), cents), :]
    best_buf[me_c] = best_ref[...]
    for copy in blocks:
        copy.wait_recv()
    total = part_buf[0]
    for g in range(1, groups):
        total = total + part_buf[g]
    for c in range(cents):
        sum_buf[c] = total[c : c + 1, :]
    row_buf[me_c] = sum_buf[me_c]
    for copy in lines:
        copy.start()

    for copy in tops:
        copy.wait_recv()
    top = best_buf[0]
    for c in range(1, cents):
        top = jnp.maximum(top, best_buf[c])
    width = token_ref.shape[1]
    for r in range(token_ref.shape[0]):
        token_ref[r : r + 1, :] = top[:, r * width : (r + 1) * width]

    for copy in lines:
        copy.wait_recv()
    line = row_buf[0]
    for c in range(1, cents):
        line = line + row_buf[c]
    half = score_ref.shape[1]
    score_ref[0:1, :] = line[:, 0:half]
    score_ref[1:2, :] = line[:, half : 2 * half]
    for copy in blocks + tops + lines:
        copy.wait_send()


def shards(queries, centroids, candidates, token_codes, resid_words, lengths, levels):
    query_rows, qtok, width = queries.shape
    cent_dev = centroids.shape[0]
    pass_dev, plen = token_codes.shape
    packed = resid_words.shape[1]
    per_device, cand_count = candidates.shape[2:]
    cents, groups = lax.axis_size("cent"), lax.axis_size("grp")
    srcs = cents * groups
    tokens = query_rows * qtok
    block, head = 4096, cent_dev // 2
    tiles = tokens // 256
    mib = 1 << 20
    dma = pltpu.SemaphoreType.DMA
    f32, i32, bf16 = jnp.float32, jnp.int32, jnp.bfloat16
    sds = jax.ShapeDtypeStruct
    hbm = functools.partial(pltpu.with_memory_space_constraint, memory_space=pltpu.HBM)

    table, tail, words, qall, qt, acc, picks, ends, entries = pl.pallas_call(
        functools.partial(search_kernel, cents, groups, pass_dev, block, head, cand_count),
        out_shape=(
            sds((cent_dev, width), f32),
            sds((cent_dev - head, width), bf16),
            sds((pass_dev, packed, width), i32),
            sds((groups, tokens, width), bf16),
            sds((tiles, width, 256), bf16),
            sds((tiles, 8, 256), f32),
            sds((32, plen // 32 * pass_dev), i32),
            sds((srcs, srcs), f32),
            sds((8, srcs), i32),
        ),
        in_specs=[VMEM, VMEM, VMEM, ANY, ANY],
        out_specs=(VMEM,) * 9,
        scratch_shapes=[
            pltpu.VMEM((head, width), bf16),
            pltpu.VMEM((cents, 1, srcs), i32),
            pltpu.VMEM((groups, cents, 1, srcs), i32),
            pltpu.VMEM((srcs, srcs), i32),
            dma((2, head // block)),
            dma,
            dma,
            dma((cents,)),
            dma((cents,)),
            dma((groups,)),
            dma((groups,)),
            dma((9,)),
            dma((9,)),
        ],
        compiler_params=pltpu.CompilerParams(
            collective_id=0, has_side_effects=True, vmem_limit_bytes=8 * mib
        ),
        name="search",
    )(
        queries.reshape(tokens, width),
        candidates.reshape(per_device, cand_count),
        token_codes,
        hbm(centroids),
        hbm(resid_words),
    )

    slots = 2 * srcs
    parts, best = pl.pallas_call(
        functools.partial(passage_kernel, cents, groups, pass_dev, plen, qtok, OPENING),
        out_shape=(sds((srcs, srcs), f32), sds((1, tokens), f32)),
        in_specs=[SMEM, SMEM, VMEM, VMEM, ANY, VMEM, VMEM, VMEM, VMEM, VMEM, VMEM],
        out_specs=(VMEM, VMEM),
        scratch_shapes=[
            pltpu.SMEM((slots + BATCH + 1,), i32),
            pltpu.VMEM((slots + BATCH, plen, width), bf16),
            pltpu.VMEM((slots + 8, 128), f32),
            pltpu.VMEM((tiles, 8, 256), f32),
            dma((32,)),
            *[pltpu.SMEM((plen // 32 * pass_dev,), i32) for _ in range(32)],
        ],
        compiler_params=pltpu.CompilerParams(vmem_limit_bytes=14 * mib),
        name="passages",
    )(
        entries,
        lengths,
        ends,
        levels,
        picks,
        table,
        tail,
        words,
        qall.reshape(groups * query_rows, qtok, width),
        qt,
        acc,
    )

    token_best, scores = pl.pallas_call(
        functools.partial(return_kernel, cents, groups),
        out_shape=(sds((query_rows, qtok), f32), sds((per_device, cand_count), f32)),
        in_specs=[VMEM, VMEM],
        out_specs=(VMEM, VMEM),
        scratch_shapes=[
            pltpu.VMEM((cents, 1, tokens), f32),
            pltpu.VMEM((groups, cents, srcs), f32),
            pltpu.VMEM((cents, 1, srcs), f32),
            pltpu.VMEM((cents, 1, srcs), f32),
            dma((cents,)),
            dma((cents,)),
            dma((groups,)),
            dma((groups,)),
            dma((cents,)),
            dma((cents,)),
        ],
        compiler_params=pltpu.CompilerParams(
            collective_id=1, has_side_effects=True, vmem_limit_bytes=4 * mib
        ),
        name="returns",
    )(best, parts)
    return token_best, scores.reshape(1, 1, per_device, cand_count)


def solution(mesh):
    placed = (
        P("grp", None, None),
        P("cent", None),
        P("grp", "cent", None, None),
        P(("cent", "grp"), None),
        P(("cent", "grp"), None, None),
        P(("cent", "grp")),
        P(),
    )
    return jax.shard_map(
        shards,
        mesh=mesh,
        in_specs=placed,
        out_specs=(P("grp", None), P("grp", "cent", None, None)),
        check_vma=False,
    )
```

```python
import functools

import jax
import jax.numpy as jnp
from jax import lax
from jax.experimental import pallas as pl
from jax.experimental.pallas import tpu as pltpu
from jax.sharding import PartitionSpec as P

MESH = pl.DeviceIdType.MESH
ANY = pl.BlockSpec(memory_space=pl.ANY)
VMEM = pl.BlockSpec(memory_space=pltpu.VMEM)
SMEM = pl.BlockSpec(memory_space=pltpu.SMEM)
EMPTY = 1 << 20
MASKED = -1000000000.0
UNITS = 8
BATCH = 16
PIECE = 1024
OPENING = 16


def greet(axis_peers):
    barrier = pltpu.get_barrier_semaphore()
    total = 0
    for axis, me, size in axis_peers:
        for d in range(1, size):
            pl.semaphore_signal(
                barrier, inc=1, device_id={axis: lax.rem(me + d, size)}, device_id_type=MESH
            )
            total += 1
    pl.semaphore_wait(barrier, total)


def push(src, dst, send, recv, axis, peer):
    return pltpu.make_async_remote_copy(
        src_ref=src,
        dst_ref=dst,
        send_sem=send,
        recv_sem=recv,
        device_id={axis: peer},
        device_id_type=MESH,
    )


def search_kernel(
    cents, groups, pass_dev, block, head, cand_count,
    q_hbm, cand_hbm, codes_hbm, cent_hbm, words_hbm,
    table_ref, tail_ref, words_ref, qall_ref, qt_ref, acc_ref, picks_ref, ends_ref, entry_ref,
    cand_ref, codes_ref, head_buf, row_buf, all_buf, rows, csem, tsem, wsem, own_sem, cand_sem, codes_sem, s1, r1, s2, r2, sq, rq,
):
    me_c, me_g = lax.axis_index("cent"), lax.axis_index("grp")
    partner = me_g + 1 - 2 * lax.rem(me_g, 2)
    ahead, behind = lax.rem(me_g + 2, groups), lax.rem(me_g + groups - 2, groups)
    across = lax.rem(me_g + 4, groups)
    steps = head // block
    later = tail_ref.shape[0] // block
    tiles, width = qt_ref.shape[0], qt_ref.shape[2]
    half = q_hbm.shape[0] // 2
    mine_q = qall_ref.at[me_g]

    cand_copy = pltpu.make_async_copy(cand_hbm, cand_ref, cand_sem)
    cand_copy.start()
    own = pltpu.make_async_copy(q_hbm, mine_q, own_sem)
    own.start()
    fetch = [
        pltpu.make_async_copy(
            cent_hbm.at[pl.ds(b * block, block)], head_buf.at[pl.ds(b * block, block)], csem.at[b]
        )
        for b in range(steps)
    ]
    fetch_tail = [
        pltpu.make_async_copy(
            cent_hbm.at[pl.ds(head + b * block, block)], tail_ref.at[pl.ds(b * block, block)], tsem.at[b]
        )
        for b in range(later)
    ]
    fetch[0].start()
    codes_copy = pltpu.make_async_copy(codes_hbm, codes_ref, codes_sem)
    codes_copy.start()
    for copy in fetch[1:] + fetch_tail:
        copy.start()
    words_copy = pltpu.make_async_copy(words_hbm, words_ref, wsem)
    words_copy.start()
    cand_copy.wait()
    row_buf[me_c] = jnp.concatenate([cand_ref[0:1, :], cand_ref[1:2, :]], axis=1)
    greet((("cent", me_c, cents), ("grp", me_g, groups)))

    gather_rows = [
        push(row_buf.at[me_c], row_buf.at[me_c], s1.at[d], r1.at[d], "cent", lax.rem(me_c + d, cents))
        for d in range(1, cents)
    ]
    gather_groups = [
        push(row_buf, all_buf.at[me_g], s2.at[d], r2.at[d], "grp", lax.rem(me_g + d, groups))
        for d in range(1, groups)
    ]

    def hand(k, block_of, peer, start=0, size=2 * half):
        held = qall_ref.at[block_of, pl.ds(start, size)]
        return push(held, held, sq.at[k], rq.at[k], "grp", peer)

    to_ahead = push(mine_q, mine_q, sq.at[0], rq.at[0], "grp", ahead)
    to_behind = push(mine_q, mine_q, sq.at[1], rq.at[1], "grp", behind)
    to_partner = push(mine_q, mine_q, sq.at[2], rq.at[2], "grp", partner)
    relay_ahead = hand(3, behind, ahead, 0, half)
    relay_behind = hand(4, ahead, behind, half, half)
    share_behind = hand(5, behind, partner)
    share_ahead = hand(6, ahead, partner)
    share_low = hand(7, across, partner, 0, half)
    share_high = hand(8, across, partner, half, half)

    for copy in gather_rows:
        copy.start()
    own.wait()
    to_ahead.start()
    to_behind.start()
    to_partner.start()

    for t in range(tiles):
        qt_ref[t] = qall_ref[me_g, t * width : (t + 1) * width, :].T
    acc_ref[...] = jnp.full(acc_ref.shape, -jnp.inf, jnp.float32)
    codes_copy.wait()
    by_token = codes_ref[...].T
    for part in range(codes_ref.shape[1] // 32):
        span = slice(part * pass_dev, (part + 1) * pass_dev)
        picks_ref[:, span] = by_token[part * 32 : (part + 1) * 32, :]

    def step(b, _):
        here = pl.ds(pl.multiple_of(b * block, block), block)
        pltpu.make_async_copy(cent_hbm.at[here], head_buf.at[here], csem.at[b]).wait()

        @pl.when(b == 1)
        def _():
            for copy in gather_rows:
                copy.wait_recv()
            for copy in gather_groups:
                copy.start()

        @pl.when(b == 2)
        def _():
            to_ahead.wait_recv()
            relay_ahead.start()
            share_behind.start()
            to_behind.wait_recv()
            relay_behind.start()
            share_ahead.start()

        table_ref[here, :] = head_buf[here, :].astype(jnp.float32)
        for t in range(tiles):
            scores = jnp.dot(head_buf[here, :], qt_ref[t], preferred_element_type=jnp.float32)
            top = jnp.max(scores.reshape(block // 8, 8, width), axis=0)
            acc_ref[t] = jnp.maximum(acc_ref[t], top)
        return 0

    lax.fori_loop(0, steps, step, 0)
    for copy in fetch_tail:
        copy.wait()
    part_rows = 1024

    def widen(r, _):
        src = pl.ds(pl.multiple_of(r * part_rows, part_rows), part_rows)
        dst = pl.ds(pl.multiple_of(head + r * part_rows, part_rows), part_rows)
        table_ref[dst, :] = tail_ref[src, :].astype(jnp.float32)
        return 0

    lax.fori_loop(0, tail_ref.shape[0] // part_rows, widen, 0)

    relay_ahead.wait_recv()
    share_low.start()
    relay_behind.wait_recv()
    share_high.start()
    for copy in gather_groups:
        copy.wait_recv()
    all_buf[me_g] = row_buf[...]
    for g in range(groups):
        for c in range(cents):
            rows[pl.ds(g * cents + c, 1), :] = all_buf[g, c]
    found = rows[...]
    lane = lax.broadcasted_iota(jnp.int32, found.shape, 1)
    mine = jnp.right_shift(found, pass_dev.bit_length() - 1) == me_c * groups + me_g
    packed = (lane * pass_dev + jnp.bitwise_and(found, pass_dev - 1)).astype(jnp.float32)
    first = jnp.min(jnp.where(mine, packed, float(EMPTY)), axis=1, keepdims=True)
    last = jnp.max(jnp.where(mine, packed, -1.0), axis=1, keepdims=True)
    ends = jnp.where(lane == 0, first, jnp.where(lane == 1, last, 0.0))
    ends_ref[...] = ends
    turned = ends.T[0:8, :].astype(jnp.int32)
    source = lax.broadcasted_iota(jnp.int32, turned.shape, 1)
    slot = lax.broadcasted_iota(jnp.int32, turned.shape, 0)
    other = jnp.where(slot == 1, jnp.broadcast_to(turned[0:1, :], turned.shape), -1)
    there = (turned < EMPTY) & (turned > other)
    query = 2 * source + jnp.right_shift(turned, (pass_dev * cand_count).bit_length() - 1)
    entry = jnp.bitwise_and(turned, pass_dev - 1) + pass_dev * (
        query + 2 * cents * groups * (slot * cents * groups + source)
    )
    entry_ref[...] = jnp.where(there, entry, -1)

    words_copy.wait()
    for copy in gather_rows + gather_groups:
        copy.wait_send()
    for copy in (to_ahead, to_behind, relay_ahead, relay_behind):
        copy.wait_send()
    for copy in (to_partner, share_behind, share_ahead, share_low, share_high):
        copy.wait()


def passage_kernel(
    cents, groups, pass_dev, plen, qtok, opening,
    entries, len_ref, ends_ref, lev_ref, picks_ref, table, tail, words, q_ref, qt_ref, acc_in,
    out_ref, best_ref,
    items, starts, units, embeds, totals, acc, spread, csem, *picks,
):
    srcs = groups * cents
    tiles = qt_ref.shape[0]
    rows_of_piece = PIECE
    pieces = tail.shape[0] // rows_of_piece * tiles
    loads = [
        pltpu.make_async_copy(picks_ref.at[r], picks[r], csem.at[r]) for r in range(len(picks))
    ]
    for copy in loads:
        copy.start()
    acc[...] = acc_in[...]

    def piece(m):
        t = lax.rem(m, tiles)
        start = pl.multiple_of(m // tiles * rows_of_piece, rows_of_piece)
        scores = jnp.dot(
            tail[pl.ds(start, rows_of_piece), :], qt_ref[t], preferred_element_type=jnp.float32
        )
        top = jnp.max(scores.reshape(rows_of_piece // 8, 8, scores.shape[1]), axis=0)
        acc[t] = jnp.maximum(acc[t], top)

    def collect(src, state):
        count, used = state
        for slot in range(2):
            entry = entries[slot, src]
            passage = jnp.bitwise_and(entry, pass_dev - 1)
            parts = jnp.right_shift(len_ref[passage] + 31, 5)
            items[count] = entry
            starts[count] = used
            for part in range(plen // 32):
                units[used + part] = passage + part * pass_dev
            there = entry >= 0
            count = count + jnp.where(there, 1, 0)
            used = used + jnp.where(there, parts, 0)
        return count, used

    def open_step(m, state):
        piece(m)
        for k in range(srcs // opening):
            state = collect(m * (srcs // opening) + k, state)
        return state

    for k in range(len(spread)):
        spread[k][...] = jnp.zeros(spread[k].shape, spread[k].dtype)
    count, used = lax.fori_loop(0, opening, open_step, (jnp.int32(0), jnp.int32(0)))
    for pad in range(BATCH):
        items[count + pad] = 2 * srcs * (2 * srcs) * pass_dev
        starts[count + pad] = 0
    for pad in range(UNITS):
        units[used + pad] = 0
    totals[...] = jnp.zeros(totals.shape, jnp.float32)
    for copy in loads:
        copy.wait()

    sub = lax.broadcasted_iota(jnp.int32, (8, 128), 0)
    level = [jnp.broadcast_to(lev_ref[k : k + 1, :], (8, 128)) for k in range(4)]

    def embed(at):
        passage = jnp.bitwise_and(at, pass_dev - 1)
        part = jnp.right_shift(at, pass_dev.bit_length() - 1)
        word = words[passage, pl.ds(pl.multiple_of(part * 8, 8), 8), :]
        tiles = []
        for j in range(4):
            rows = None
            for s in range(8):
                row = table[pl.ds(picks[4 * s + j][at], 1), :]
                row = jnp.broadcast_to(row, (8, 128))
                rows = row if rows is None else jnp.where(sub == s, row, rows)
            low = jnp.bitwise_and(word, 1 << (2 * j)) != 0
            high = jnp.bitwise_and(word, 2 << (2 * j)) != 0
            residual = jnp.where(
                high, jnp.where(low, level[3], level[2]), jnp.where(low, level[1], level[0])
            )
            dense = rows + residual
            squares = jnp.sum(dense * dense, axis=1, keepdims=True)
            tiles.append(dense * lax.rsqrt(squares + 1e-06))
        return jnp.concatenate(tiles, axis=0).astype(jnp.bfloat16)

    def embed_step(i, _):
        values = [embed(units[i * UNITS + k]) for k in range(UNITS)]
        for k, value in enumerate(values):
            embeds[pl.ds(pl.multiple_of(i * (UNITS * 32) + k * 32, 32), 32), :] = value
        return 0

    def piece_step(m, _):
        piece(m)
        return 0

    def both_step(i, _):
        piece(opening + i)
        return embed_step(i, 0)

    turns = pl.cdiv(used, UNITS)
    shared = jnp.minimum(turns, pieces - opening)
    lax.fori_loop(0, shared, both_step, 0)
    lax.fori_loop(shared, turns, embed_step, 0)
    lax.fori_loop(opening + shared, pieces, piece_step, 0)
    embeds[pl.ds(pl.multiple_of(turns * (UNITS * 32), 32), plen), :] = jnp.zeros(
        (plen, embeds.shape[1]), embeds.dtype
    )
    for t in range(tiles):
        width = acc.shape[2]
        best_ref[:, t * width : (t + 1) * width] = jnp.max(acc[t], axis=0, keepdims=True)

    lane_q = lax.broadcasted_iota(jnp.int32, (8, 128), 1)
    four = 128 // qtok

    def score_step(batch, _):
        for k, wide in enumerate(spread):
            limit, rows, held = None, [], []
            for n in range(four):
                i = batch * BATCH + k * four + n
                entry = items[i]
                query = jnp.bitwise_and(jnp.right_shift(entry, pass_dev.bit_length() - 1), 2 * srcs - 1)
                rows.append(jnp.right_shift(entry, (2 * srcs * pass_dev).bit_length() - 1))
                length = len_ref[jnp.bitwise_and(entry, pass_dev - 1)]
                wide[n * qtok : (n + 1) * qtok, n * 128 : (n + 1) * 128] = q_ref[query]
                limit = length if limit is None else jnp.where(lane_q >= n * qtok, length, limit)
                held.append(embeds[pl.ds(pl.multiple_of(starts[i] * 32, 32), plen), :])
            scores = lax.dot_general(
                jnp.concatenate(held, axis=1), wide[...], (((1,), (1,)), ((), ())), preferred_element_type=jnp.float32
            )
            top = None
            for part in range(plen // 32):
                for j in range(4):
                    at = part * 32 + j * 8
                    inside = 4 * sub + (part * 32 + j) < limit
                    tile = jnp.where(inside, scores[at : at + 8], MASKED)
                    top = tile if top is None else jnp.maximum(top, tile)
            line = jnp.max(top, axis=0, keepdims=True)
            for n in range(four):
                own = (lane_q[0:1] >= n * qtok) & (lane_q[0:1] < (n + 1) * qtok)
                totals[pl.ds(rows[n], 1), :] = jnp.where(own, line, 0.0)
        return 0

    lax.fori_loop(0, pl.cdiv(count, BATCH), score_step, 0)

    value = jnp.sum(totals[0 : 2 * srcs, :], axis=1, keepdims=True) * (1.0 / qtok)
    ends = ends_ref[...]
    lane = lax.broadcasted_iota(jnp.int32, (srcs, srcs), 1)
    place = jnp.right_shift(ends.astype(jnp.int32), pass_dev.bit_length() - 1)
    low, high = place[:, 0:1], place[:, 1:2]
    second = ends[:, 1:2] > ends[:, 0:1]
    out_ref[...] = jnp.where(lane == low, value[0:srcs], 0.0) + jnp.where(
        (lane == high) & second, value[srcs : 2 * srcs], 0.0
    )


def return_kernel(
    cents, groups,
    best_ref, part_ref,
    token_ref, score_ref,
    best_buf, part_buf, sum_buf, row_buf, sb, rb, s1, r1, s2, r2,
):
    me_c, me_g = lax.axis_index("cent"), lax.axis_index("grp")
    greet((("cent", me_c, cents), ("grp", me_g, groups)))

    def rows_of(g):
        return part_ref.at[pl.ds(pl.multiple_of(g * cents, cents), cents)]

    blocks, tops, lines = [], [], []
    for d in range(1, groups):
        peer = lax.rem(me_g + d, groups)
        blocks.append(push(rows_of(peer), part_buf.at[me_g], s1.at[d], r1.at[d], "grp", peer))
    for d in range(1, cents):
        peer = lax.rem(me_c + d, cents)
        tops.append(push(best_ref, best_buf.at[me_c], sb.at[d], rb.at[d], "cent", peer))
        lines.append(push(sum_buf.at[peer], row_buf.at[me_c], s2.at[d], r2.at[d], "cent", peer))
    for copy in blocks:
        copy.start()
    for copy in tops:
        copy.start()
    part_buf[me_g] = part_ref[pl.ds(pl.multiple_of(me_g * cents, cents), cents), :]
    best_buf[me_c] = best_ref[...]
    for copy in blocks:
        copy.wait_recv()
    total = part_buf[0]
    for g in range(1, groups):
        total = total + part_buf[g]
    for c in range(cents):
        sum_buf[c] = total[c : c + 1, :]
    row_buf[me_c] = sum_buf[me_c]
    for copy in lines:
        copy.start()

    for copy in tops:
        copy.wait_recv()
    top = best_buf[0]
    for c in range(1, cents):
        top = jnp.maximum(top, best_buf[c])
    width = token_ref.shape[1]
    for r in range(token_ref.shape[0]):
        token_ref[r : r + 1, :] = top[:, r * width : (r + 1) * width]

    for copy in lines:
        copy.wait_recv()
    line = row_buf[0]
    for c in range(1, cents):
        line = line + row_buf[c]
    half = score_ref.shape[1]
    score_ref[0:1, :] = line[:, 0:half]
    score_ref[1:2, :] = line[:, half : 2 * half]
    for copy in blocks + tops + lines:
        copy.wait_send()


def shards(queries, centroids, candidates, token_codes, resid_words, lengths, levels):
    query_rows, qtok, width = queries.shape
    cent_dev = centroids.shape[0]
    pass_dev, plen = token_codes.shape
    packed = resid_words.shape[1]
    per_device, cand_count = candidates.shape[2:]
    cents, groups = lax.axis_size("cent"), lax.axis_size("grp")
    srcs = cents * groups
    tokens = query_rows * qtok
    block, head = 4096, 3 * cent_dev // 8
    tiles = tokens // 256
    mib = 1 << 20
    dma = pltpu.SemaphoreType.DMA
    f32, i32, bf16 = jnp.float32, jnp.int32, jnp.bfloat16
    sds = jax.ShapeDtypeStruct
    hbm = functools.partial(pltpu.with_memory_space_constraint, memory_space=pltpu.HBM)

    table, tail, words, qall, qt, acc, picks, ends, entries = pl.pallas_call(
        functools.partial(search_kernel, cents, groups, pass_dev, block, head, cand_count),
        out_shape=(
            sds((cent_dev, width), f32),
            sds((cent_dev - head, width), bf16),
            sds((pass_dev, packed, width), i32),
            sds((groups, tokens, width), bf16),
            sds((tiles, width, 256), bf16),
            sds((tiles, 8, 256), f32),
            sds((32, plen // 32 * pass_dev), i32),
            sds((srcs, srcs), f32),
            sds((8, srcs), i32),
        ),
        in_specs=[ANY] * 5,
        out_specs=(VMEM,) * 9,
        scratch_shapes=[
            pltpu.VMEM((per_device, cand_count), i32),
            pltpu.VMEM((pass_dev, plen), i32),
            pltpu.VMEM((head, width), bf16),
            pltpu.VMEM((cents, 1, srcs), i32),
            pltpu.VMEM((groups, cents, 1, srcs), i32),
            pltpu.VMEM((srcs, srcs), i32),
            dma((head // block,)),
            dma(((cent_dev - head) // block,)),
            dma,
            dma,
            dma,
            dma,
            dma((cents,)),
            dma((cents,)),
            dma((groups,)),
            dma((groups,)),
            dma((9,)),
            dma((9,)),
        ],
        compiler_params=pltpu.CompilerParams(
            collective_id=0, has_side_effects=True, vmem_limit_bytes=8 * mib
        ),
        name="search",
    )(
        hbm(queries.reshape(tokens, width)),
        hbm(candidates.reshape(per_device, cand_count)),
        hbm(token_codes),
        hbm(centroids),
        hbm(resid_words),
    )

    slots = 2 * srcs
    parts, best = pl.pallas_call(
        functools.partial(passage_kernel, cents, groups, pass_dev, plen, qtok, OPENING),
        out_shape=(sds((srcs, srcs), f32), sds((1, tokens), f32)),
        in_specs=[SMEM, SMEM, VMEM, VMEM, ANY, VMEM, VMEM, VMEM, VMEM, VMEM, VMEM],
        out_specs=(VMEM, VMEM),
        scratch_shapes=[
            pltpu.SMEM((slots + BATCH,), i32),
            pltpu.SMEM((slots + BATCH,), i32),
            pltpu.SMEM((slots * (plen // 32) + UNITS + 4,), i32),
            pltpu.VMEM((slots * plen + UNITS * 32 + plen, width), bf16),
            pltpu.VMEM((slots + 8, 128), f32),
            pltpu.VMEM((tiles, 8, 256), f32),
            [pltpu.VMEM((128, 128 // qtok * width), bf16) for _ in range(BATCH * qtok // 128)],
            dma((32,)),
            *[pltpu.SMEM((plen // 32 * pass_dev,), i32) for _ in range(32)],
        ],
        compiler_params=pltpu.CompilerParams(vmem_limit_bytes=14 * mib),
        name="passages",
    )(
        entries,
        lengths,
        ends,
        levels,
        picks,
        table,
        tail,
        words,
        qall.reshape(groups * query_rows, qtok, width),
        qt,
        acc,
    )

    token_best, scores = pl.pallas_call(
        functools.partial(return_kernel, cents, groups),
        out_shape=(sds((query_rows, qtok), f32), sds((per_device, cand_count), f32)),
        in_specs=[VMEM, VMEM],
        out_specs=(VMEM, VMEM),
        scratch_shapes=[
            pltpu.VMEM((cents, 1, tokens), f32),
            pltpu.VMEM((groups, cents, srcs), f32),
            pltpu.VMEM((cents, 1, srcs), f32),
            pltpu.VMEM((cents, 1, srcs), f32),
            dma((cents,)),
            dma((cents,)),
            dma((groups,)),
            dma((groups,)),
            dma((cents,)),
            dma((cents,)),
        ],
        compiler_params=pltpu.CompilerParams(
            collective_id=1, has_side_effects=True, vmem_limit_bytes=4 * mib
        ),
        name="returns",
    )(best, parts)
    return token_best, scores.reshape(1, 1, per_device, cand_count)


def solution(mesh):
    placed = (
        P("grp", None, None),
        P("cent", None),
        P("grp", "cent", None, None),
        P(("cent", "grp"), None),
        P(("cent", "grp"), None, None),
        P(("cent", "grp")),
        P(),
    )
    return jax.shard_map(
        shards,
        mesh=mesh,
        in_specs=placed,
        out_specs=(P("grp", None), P("grp", "cent", None, None)),
        check_vma=False,
    )
```

```python
import functools

import jax
import jax.numpy as jnp
from jax import lax
from jax.experimental import pallas as pl
from jax.experimental.pallas import tpu as pltpu
from jax.sharding import PartitionSpec as P

MESH = pl.DeviceIdType.MESH
ANY = pl.BlockSpec(memory_space=pl.ANY)
VMEM = pl.BlockSpec(memory_space=pltpu.VMEM)
SMEM = pl.BlockSpec(memory_space=pltpu.SMEM)
EMPTY = 1 << 20
MASKED = -1000000000.0
UNITS = 8
BATCH = 32
PIECE = 1024
OPENING = 16


def greet(axis_peers):
    barrier = pltpu.get_barrier_semaphore()
    total = 0
    for axis, me, size in axis_peers:
        for d in range(1, size):
            pl.semaphore_signal(
                barrier, inc=1, device_id={axis: lax.rem(me + d, size)}, device_id_type=MESH
            )
            total += 1
    pl.semaphore_wait(barrier, total)


def push(src, dst, send, recv, axis, peer):
    return pltpu.make_async_remote_copy(
        src_ref=src,
        dst_ref=dst,
        send_sem=send,
        recv_sem=recv,
        device_id={axis: peer},
        device_id_type=MESH,
    )


def search_kernel(
    cents, groups, pass_dev, block, head, cand_count,
    q_hbm, cand_hbm, codes_hbm, cent_hbm, words_hbm,
    table_ref, tail_ref, words_ref, qall_ref, qt_ref, acc_ref, picks_ref, ends_ref, entry_ref,
    cand_ref, codes_ref, head_buf, row_buf, all_buf, rows, csem, tsem, wsem, own_sem, cand_sem, codes_sem, s1, r1, s2, r2, sq, rq,
):
    me_c, me_g = lax.axis_index("cent"), lax.axis_index("grp")
    partner = me_g + 1 - 2 * lax.rem(me_g, 2)
    ahead, behind = lax.rem(me_g + 2, groups), lax.rem(me_g + groups - 2, groups)
    across = lax.rem(me_g + 4, groups)
    steps = head // block
    later = tail_ref.shape[0] // block
    tiles, width = qt_ref.shape[0], qt_ref.shape[2]
    half = q_hbm.shape[0] // 2
    mine_q = qall_ref.at[me_g]

    cand_copy = pltpu.make_async_copy(cand_hbm, cand_ref, cand_sem)
    cand_copy.start()
    own = pltpu.make_async_copy(q_hbm, mine_q, own_sem)
    own.start()
    fetch = [
        pltpu.make_async_copy(
            cent_hbm.at[pl.ds(b * block, block)], head_buf.at[pl.ds(b * block, block)], csem.at[b]
        )
        for b in range(steps)
    ]
    fetch_tail = [
        pltpu.make_async_copy(
            cent_hbm.at[pl.ds(head + b * block, block)], tail_ref.at[pl.ds(b * block, block)], tsem.at[b]
        )
        for b in range(later)
    ]
    fetch[0].start()
    codes_copy = pltpu.make_async_copy(codes_hbm, codes_ref, codes_sem)
    codes_copy.start()
    for copy in fetch[1:] + fetch_tail:
        copy.start()
    words_copy = pltpu.make_async_copy(words_hbm, words_ref, wsem)
    words_copy.start()
    cand_copy.wait()
    row_buf[me_c] = jnp.concatenate([cand_ref[0:1, :], cand_ref[1:2, :]], axis=1)
    greet((("cent", me_c, cents), ("grp", me_g, groups)))

    gather_rows = [
        push(row_buf.at[me_c], row_buf.at[me_c], s1.at[d], r1.at[d], "cent", lax.rem(me_c + d, cents))
        for d in range(1, cents)
    ]
    gather_groups = [
        push(row_buf, all_buf.at[me_g], s2.at[d], r2.at[d], "grp", lax.rem(me_g + d, groups))
        for d in range(1, groups)
    ]

    low, high = pl.ds(0, half), pl.ds(half, half)
    lanes = iter(range(sq.shape[0]))

    def hand(block_of, span, peer):
        k = next(lanes)
        held = qall_ref.at[block_of, span]
        return push(held, held, sq.at[k], rq.at[k], "grp", peer)

    ahead_low, behind_high = hand(me_g, low, ahead), hand(me_g, high, behind)
    ahead_high, behind_low = hand(me_g, high, ahead), hand(me_g, low, behind)
    to_partner = hand(me_g, pl.ds(0, 2 * half), partner)
    relay_ahead, relay_behind = hand(behind, low, ahead), hand(ahead, high, behind)
    shares = [
        hand(block_of, span, partner)
        for block_of, span in (
            (behind, low), (ahead, high), (behind, high), (ahead, low), (across, low), (across, high)
        )
    ]

    for copy in gather_rows:
        copy.start()
    own.wait()
    for copy in (ahead_low, behind_high, ahead_high, behind_low, to_partner):
        copy.start()

    for t in range(tiles):
        qt_ref[t] = qall_ref[me_g, t * width : (t + 1) * width, :].T
    acc_ref[...] = jnp.full(acc_ref.shape, -jnp.inf, jnp.float32)
    codes_copy.wait()
    by_token = codes_ref[...].T
    for part in range(codes_ref.shape[1] // 32):
        span = slice(part * pass_dev, (part + 1) * pass_dev)
        picks_ref[:, span] = by_token[part * 32 : (part + 1) * 32, :]

    def step(b, _):
        here = pl.ds(pl.multiple_of(b * block, block), block)
        pltpu.make_async_copy(cent_hbm.at[here], head_buf.at[here], csem.at[b]).wait()

        @pl.when(b == 2)
        def _():
            for copy in gather_rows:
                copy.wait_recv()
            for copy in gather_groups:
                copy.start()

        @pl.when(b == 3)
        def _():
            ahead_low.wait_recv()
            relay_ahead.start()
            shares[0].start()
            behind_high.wait_recv()
            relay_behind.start()
            shares[1].start()

        @pl.when(b == 6)
        def _():
            ahead_high.wait_recv()
            shares[2].start()
            behind_low.wait_recv()
            shares[3].start()

        table_ref[here, :] = head_buf[here, :].astype(jnp.float32)
        for t in range(tiles):
            scores = jnp.dot(head_buf[here, :], qt_ref[t], preferred_element_type=jnp.float32)
            top = jnp.max(scores.reshape(block // 8, 8, width), axis=0)
            acc_ref[t] = jnp.maximum(acc_ref[t], top)
        return 0

    lax.fori_loop(0, steps, step, 0)
    for copy in fetch_tail:
        copy.wait()
    part_rows = 1024

    def widen(r, _):
        src = pl.ds(pl.multiple_of(r * part_rows, part_rows), part_rows)
        dst = pl.ds(pl.multiple_of(head + r * part_rows, part_rows), part_rows)
        table_ref[dst, :] = tail_ref[src, :].astype(jnp.float32)
        return 0

    lax.fori_loop(0, tail_ref.shape[0] // part_rows, widen, 0)

    relay_ahead.wait_recv()
    shares[4].start()
    relay_behind.wait_recv()
    shares[5].start()
    for copy in gather_groups:
        copy.wait_recv()
    all_buf[me_g] = row_buf[...]
    for g in range(groups):
        for c in range(cents):
            rows[pl.ds(g * cents + c, 1), :] = all_buf[g, c]
    found = rows[...]
    lane = lax.broadcasted_iota(jnp.int32, found.shape, 1)
    mine = jnp.right_shift(found, pass_dev.bit_length() - 1) == me_c * groups + me_g
    packed = (lane * pass_dev + jnp.bitwise_and(found, pass_dev - 1)).astype(jnp.float32)
    first = jnp.min(jnp.where(mine, packed, float(EMPTY)), axis=1, keepdims=True)
    last = jnp.max(jnp.where(mine, packed, -1.0), axis=1, keepdims=True)
    ends = jnp.where(lane == 0, first, jnp.where(lane == 1, last, 0.0))
    ends_ref[...] = ends
    turned = ends.T[0:8, :].astype(jnp.int32)
    source = lax.broadcasted_iota(jnp.int32, turned.shape, 1)
    slot = lax.broadcasted_iota(jnp.int32, turned.shape, 0)
    other = jnp.where(slot == 1, jnp.broadcast_to(turned[0:1, :], turned.shape), -1)
    there = (turned < EMPTY) & (turned > other)
    query = 2 * source + jnp.right_shift(turned, (pass_dev * cand_count).bit_length() - 1)
    entry = jnp.bitwise_and(turned, pass_dev - 1) + pass_dev * (
        query + 2 * cents * groups * (slot * cents * groups + source)
    )
    entry_ref[...] = jnp.where(there, entry, -1)

    words_copy.wait()
    for copy in gather_rows + gather_groups:
        copy.wait_send()
    for copy in (ahead_low, behind_high, ahead_high, behind_low, relay_ahead, relay_behind):
        copy.wait_send()
    for copy in [to_partner] + shares:
        copy.wait()


def passage_kernel(
    cents, groups, pass_dev, plen, qtok, opening,
    entries, len_ref, ends_ref, lev_ref, picks_ref, table, tail, words, q_ref, qt_ref, acc_in,
    out_ref, best_ref,
    items, starts, units, seen, embeds, totals, acc, spread, csem, *picks,
):
    srcs = groups * cents
    tiles = qt_ref.shape[0]
    rows_of_piece = PIECE
    pieces = tail.shape[0] // rows_of_piece * tiles
    loads = [
        pltpu.make_async_copy(picks_ref.at[r], picks[r], csem.at[r]) for r in range(len(picks))
    ]
    for copy in loads:
        copy.start()
    acc[...] = acc_in[...]

    def piece(m):
        t = lax.rem(m, tiles)
        start = pl.multiple_of(m // tiles * rows_of_piece, rows_of_piece)
        scores = jnp.dot(
            tail[pl.ds(start, rows_of_piece), :], qt_ref[t], preferred_element_type=jnp.float32
        )
        top = jnp.max(scores.reshape(rows_of_piece // 8, 8, scores.shape[1]), axis=0)
        acc[t] = jnp.maximum(acc[t], top)

    def collect(src, state):
        count, used = state
        pair = [entries[slot * srcs + src] for slot in range(2)]
        there = [entry >= 0 for entry in pair]
        owned = [jnp.bitwise_and(entry, pass_dev - 1) for entry in pair]
        marks = [jnp.where(ok, passage, pass_dev) for ok, passage in zip(there, owned)]
        known = [seen[mark] for mark in marks]
        sizes = [jnp.right_shift(len_ref[passage] + 31, 5) for passage in owned]
        for n in range(2):
            at = jnp.where(known[n] < 0, used, known[n])
            items[count] = pair[n]
            starts[count] = at
            seen[marks[n]] = at
            for part in range(plen // 32):
                units[used + part] = owned[n] + part * pass_dev
            count = count + jnp.where(there[n], 1, 0)
            used = used + jnp.where(there[n] & (known[n] < 0), sizes[n], 0)
        return count, used

    def open_step(m, state):
        piece(m)
        for k in range(srcs // opening):
            state = collect(m * (srcs // opening) + k, state)
        return state

    for k in range(len(spread)):
        spread[k][...] = jnp.zeros(spread[k].shape, spread[k].dtype)
    def forget(k, _):
        seen[k] = -1
        return 0

    lax.fori_loop(0, pass_dev, forget, 0, unroll=16)
    count, used = lax.fori_loop(0, opening, open_step, (jnp.int32(0), jnp.int32(0)))
    for pad in range(BATCH):
        items[count + pad] = 2 * srcs * (2 * srcs) * pass_dev
        starts[count + pad] = 0
    for pad in range(UNITS):
        units[used + pad] = 0
    totals[...] = jnp.zeros(totals.shape, jnp.float32)
    for copy in loads:
        copy.wait()

    sub = lax.broadcasted_iota(jnp.int32, (8, 128), 0)
    level = [jnp.broadcast_to(lev_ref[k : k + 1, :], (8, 128)) for k in range(4)]

    def embed(at):
        passage = jnp.bitwise_and(at, pass_dev - 1)
        part = jnp.right_shift(at, pass_dev.bit_length() - 1)
        word = words[passage, pl.ds(pl.multiple_of(part * 8, 8), 8), :]
        tiles = []
        for j in range(4):
            rows = None
            for s in range(8):
                row = table[pl.ds(picks[4 * s + j][at], 1), :]
                row = jnp.broadcast_to(row, (8, 128))
                rows = row if rows is None else jnp.where(sub == s, row, rows)
            low = jnp.bitwise_and(word, 1 << (2 * j)) != 0
            high = jnp.bitwise_and(word, 2 << (2 * j)) != 0
            residual = jnp.where(
                high, jnp.where(low, level[3], level[2]), jnp.where(low, level[1], level[0])
            )
            dense = rows + residual
            squares = jnp.sum(dense * dense, axis=1, keepdims=True)
            tiles.append(dense * lax.rsqrt(squares + 1e-06))
        return jnp.concatenate(tiles, axis=0).astype(jnp.bfloat16)

    def embed_step(i, _):
        values = [embed(units[i * UNITS + k]) for k in range(UNITS)]
        for k, value in enumerate(values):
            embeds[pl.ds(pl.multiple_of(i * (UNITS * 32) + k * 32, 32), 32), :] = value
        return 0

    def piece_step(m, _):
        piece(m)
        return 0

    def both_step(i, _):
        piece(opening + i)
        return embed_step(i, 0)

    turns = pl.cdiv(used, UNITS)
    shared = jnp.minimum(turns, pieces - opening)
    lax.fori_loop(0, shared, both_step, 0)
    lax.fori_loop(shared, turns, embed_step, 0)
    lax.fori_loop(opening + shared, pieces, piece_step, 0)
    embeds[pl.ds(pl.multiple_of(turns * (UNITS * 32), 32), plen), :] = jnp.zeros(
        (plen, embeds.shape[1]), embeds.dtype
    )
    for t in range(tiles):
        width = acc.shape[2]
        best_ref[:, t * width : (t + 1) * width] = jnp.max(acc[t], axis=0, keepdims=True)

    lane_q = lax.broadcasted_iota(jnp.int32, (8, 128), 1)
    four = 128 // qtok

    def score_step(batch, _):
        for k, wide in enumerate(spread):
            limit, rows, held = None, [], []
            for n in range(four):
                i = batch * BATCH + k * four + n
                entry = items[i]
                query = jnp.bitwise_and(jnp.right_shift(entry, pass_dev.bit_length() - 1), 2 * srcs - 1)
                rows.append(jnp.right_shift(entry, (2 * srcs * pass_dev).bit_length() - 1))
                length = len_ref[jnp.bitwise_and(entry, pass_dev - 1)]
                wide[n * qtok : (n + 1) * qtok, n * 128 : (n + 1) * 128] = q_ref[query]
                limit = length if limit is None else jnp.where(lane_q >= n * qtok, length, limit)
                held.append(embeds[pl.ds(pl.multiple_of(starts[i] * 32, 32), plen), :])
            scores = lax.dot_general(
                jnp.concatenate(held, axis=1), wide[...], (((1,), (1,)), ((), ())), preferred_element_type=jnp.float32
            )
            top = None
            for part in range(plen // 32):
                for j in range(4):
                    at = part * 32 + j * 8
                    inside = 4 * sub + (part * 32 + j) < limit
                    tile = jnp.where(inside, scores[at : at + 8], MASKED)
                    top = tile if top is None else jnp.maximum(top, tile)
            line = jnp.max(top, axis=0, keepdims=True)
            for n in range(four):
                own = (lane_q[0:1] >= n * qtok) & (lane_q[0:1] < (n + 1) * qtok)
                totals[pl.ds(rows[n], 1), :] = jnp.where(own, line, 0.0)
        return 0

    lax.fori_loop(0, pl.cdiv(count, BATCH), score_step, 0)

    value = jnp.sum(totals[0 : 2 * srcs, :], axis=1, keepdims=True) * (1.0 / qtok)
    ends = ends_ref[...]
    lane = lax.broadcasted_iota(jnp.int32, (srcs, srcs), 1)
    place = jnp.right_shift(ends.astype(jnp.int32), pass_dev.bit_length() - 1)
    low, high = place[:, 0:1], place[:, 1:2]
    second = ends[:, 1:2] > ends[:, 0:1]
    out_ref[...] = jnp.where(lane == low, value[0:srcs], 0.0) + jnp.where(
        (lane == high) & second, value[srcs : 2 * srcs], 0.0
    )


def return_kernel(
    cents, groups,
    best_ref, part_ref,
    token_ref, score_ref,
    best_buf, part_buf, sum_buf, row_buf, sb, rb, s1, r1, s2, r2,
):
    me_c, me_g = lax.axis_index("cent"), lax.axis_index("grp")
    greet((("cent", me_c, cents), ("grp", me_g, groups)))

    def rows_of(g):
        return part_ref.at[pl.ds(pl.multiple_of(g * cents, cents), cents)]

    blocks, tops, lines = [], [], []
    for d in range(1, groups):
        peer = lax.rem(me_g + d, groups)
        blocks.append(push(rows_of(peer), part_buf.at[me_g], s1.at[d], r1.at[d], "grp", peer))
    for d in range(1, cents):
        peer = lax.rem(me_c + d, cents)
        tops.append(push(best_ref, best_buf.at[me_c], sb.at[d], rb.at[d], "cent", peer))
        lines.append(push(sum_buf.at[peer], row_buf.at[me_c], s2.at[d], r2.at[d], "cent", peer))
    for copy in blocks:
        copy.start()
    for copy in tops:
        copy.start()
    part_buf[me_g] = part_ref[pl.ds(pl.multiple_of(me_g * cents, cents), cents), :]
    best_buf[me_c] = best_ref[...]
    for copy in blocks:
        copy.wait_recv()
    total = part_buf[0]
    for g in range(1, groups):
        total = total + part_buf[g]
    for c in range(cents):
        sum_buf[c] = total[c : c + 1, :]
    row_buf[me_c] = sum_buf[me_c]
    for copy in lines:
        copy.start()

    for copy in tops:
        copy.wait_recv()
    top = best_buf[0]
    for c in range(1, cents):
        top = jnp.maximum(top, best_buf[c])
    width = token_ref.shape[1]
    for r in range(token_ref.shape[0]):
        token_ref[r : r + 1, :] = top[:, r * width : (r + 1) * width]

    for copy in lines:
        copy.wait_recv()
    line = row_buf[0]
    for c in range(1, cents):
        line = line + row_buf[c]
    half = score_ref.shape[1]
    score_ref[0:1, :] = line[:, 0:half]
    score_ref[1:2, :] = line[:, half : 2 * half]
    for copy in blocks + tops + lines:
        copy.wait_send()


def shards(queries, centroids, candidates, token_codes, resid_words, lengths, levels):
    query_rows, qtok, width = queries.shape
    cent_dev = centroids.shape[0]
    pass_dev, plen = token_codes.shape
    packed = resid_words.shape[1]
    per_device, cand_count = candidates.shape[2:]
    cents, groups = lax.axis_size("cent"), lax.axis_size("grp")
    srcs = cents * groups
    tokens = query_rows * qtok
    block, head = 2048, cent_dev // 2
    tiles = tokens // 256
    mib = 1 << 20
    dma = pltpu.SemaphoreType.DMA
    f32, i32, bf16 = jnp.float32, jnp.int32, jnp.bfloat16
    sds = jax.ShapeDtypeStruct
    hbm = functools.partial(pltpu.with_memory_space_constraint, memory_space=pltpu.HBM)

    table, tail, words, qall, qt, acc, picks, ends, entries = pl.pallas_call(
        functools.partial(search_kernel, cents, groups, pass_dev, block, head, cand_count),
        out_shape=(
            sds((cent_dev, width), f32),
            sds((cent_dev - head, width), bf16),
            sds((pass_dev, packed, width), i32),
            sds((groups, tokens, width), bf16),
            sds((tiles, width, 256), bf16),
            sds((tiles, 8, 256), f32),
            sds((32, plen // 32 * pass_dev), i32),
            sds((srcs, srcs), f32),
            sds((8, srcs), i32),
        ),
        in_specs=[ANY] * 5,
        out_specs=(VMEM,) * 9,
        scratch_shapes=[
            pltpu.VMEM((per_device, cand_count), i32),
            pltpu.VMEM((pass_dev, plen), i32),
            pltpu.VMEM((head, width), bf16),
            pltpu.VMEM((cents, 1, srcs), i32),
            pltpu.VMEM((groups, cents, 1, srcs), i32),
            pltpu.VMEM((srcs, srcs), i32),
            dma((head // block,)),
            dma(((cent_dev - head) // block,)),
            dma,
            dma,
            dma,
            dma,
            dma((cents,)),
            dma((cents,)),
            dma((groups,)),
            dma((groups,)),
            dma((13,)),
            dma((13,)),
        ],
        compiler_params=pltpu.CompilerParams(
            collective_id=0, has_side_effects=True, vmem_limit_bytes=8 * mib
        ),
        name="search",
    )(
        hbm(queries.reshape(tokens, width)),
        hbm(candidates.reshape(per_device, cand_count)),
        hbm(token_codes),
        hbm(centroids),
        hbm(resid_words),
    )

    slots = 2 * srcs
    parts, best = pl.pallas_call(
        functools.partial(passage_kernel, cents, groups, pass_dev, plen, qtok, OPENING),
        out_shape=(sds((srcs, srcs), f32), sds((1, tokens), f32)),
        in_specs=[SMEM, SMEM, VMEM, VMEM, ANY, VMEM, VMEM, VMEM, VMEM, VMEM, VMEM],
        out_specs=(VMEM, VMEM),
        scratch_shapes=[
            pltpu.SMEM((slots + BATCH,), i32),
            pltpu.SMEM((slots + BATCH,), i32),
            pltpu.SMEM((slots * (plen // 32) + UNITS + 4,), i32),
            pltpu.SMEM((pass_dev + 1,), i32),
            pltpu.VMEM((slots * plen + UNITS * 32 + plen, width), bf16),
            pltpu.VMEM((slots + 8, 128), f32),
            pltpu.VMEM((tiles, 8, 256), f32),
            [pltpu.VMEM((128, 128 // qtok * width), bf16) for _ in range(BATCH * qtok // 128)],
            dma((32,)),
            *[pltpu.SMEM((plen // 32 * pass_dev,), i32) for _ in range(32)],
        ],
        compiler_params=pltpu.CompilerParams(vmem_limit_bytes=14 * mib),
        name="passages",
    )(
        entries.reshape(8 * srcs),
        lengths,
        ends,
        levels,
        picks,
        table,
        tail,
        words,
        qall.reshape(groups * query_rows, qtok, width),
        qt,
        acc,
    )

    token_best, scores = pl.pallas_call(
        functools.partial(return_kernel, cents, groups),
        out_shape=(sds((query_rows, qtok), f32), sds((per_device, cand_count), f32)),
        in_specs=[VMEM, VMEM],
        out_specs=(VMEM, VMEM),
        scratch_shapes=[
            pltpu.VMEM((cents, 1, tokens), f32),
            pltpu.VMEM((groups, cents, srcs), f32),
            pltpu.VMEM((cents, 1, srcs), f32),
            pltpu.VMEM((cents, 1, srcs), f32),
            dma((cents,)),
            dma((cents,)),
            dma((groups,)),
            dma((groups,)),
            dma((cents,)),
            dma((cents,)),
        ],
        compiler_params=pltpu.CompilerParams(
            collective_id=1, has_side_effects=True, vmem_limit_bytes=4 * mib
        ),
        name="returns",
    )(best, parts)
    return token_best, scores.reshape(1, 1, per_device, cand_count)


def solution(mesh):
    placed = (
        P("grp", None, None),
        P("cent", None),
        P("grp", "cent", None, None),
        P(("cent", "grp"), None),
        P(("cent", "grp"), None, None),
        P(("cent", "grp")),
        P(),
    )
    return jax.shard_map(
        shards,
        mesh=mesh,
        in_specs=placed,
        out_specs=(P("grp", None), P("grp", "cent", None, None)),
        check_vma=False,
    )
```

```python
import functools

import jax
import jax.numpy as jnp
from jax import lax
from jax.experimental import pallas as pl
from jax.experimental.pallas import tpu as pltpu
from jax.sharding import PartitionSpec as P

MESH = pl.DeviceIdType.MESH
ANY = pl.BlockSpec(memory_space=pl.ANY)
VMEM = pl.BlockSpec(memory_space=pltpu.VMEM)
SMEM = pl.BlockSpec(memory_space=pltpu.SMEM)
EMPTY = 1 << 20
MASKED = -1000000000.0
UNITS = 8
BATCH = 32
PIECE = 1024
OPENING = 8


def greet(axis_peers):
    barrier = pltpu.get_barrier_semaphore()
    total = 0
    for axis, me, size in axis_peers:
        for d in range(1, size):
            pl.semaphore_signal(
                barrier, inc=1, device_id={axis: lax.rem(me + d, size)}, device_id_type=MESH
            )
            total += 1
    return lambda: pl.semaphore_wait(barrier, total)


def push(src, dst, send, recv, axis, peer):
    return pltpu.make_async_remote_copy(
        src_ref=src,
        dst_ref=dst,
        send_sem=send,
        recv_sem=recv,
        device_id={axis: peer},
        device_id_type=MESH,
    )


def search_kernel(
    cents, groups, pass_dev, block, head, cand_count,
    q_hbm, cand_hbm, codes_hbm, cent_hbm, words_hbm,
    table_ref, tail_ref, words_ref, qall_ref, qt_ref, acc_ref, picks_ref, ends_ref, entry_ref,
    cand_ref, codes_ref, head_buf, row_buf, all_buf, rows, csem, tsem, wsem, own_sem, cand_sem, codes_sem, s1, r1, s2, r2, sq, rq,
):
    me_c, me_g = lax.axis_index("cent"), lax.axis_index("grp")
    partner = me_g + 1 - 2 * lax.rem(me_g, 2)
    ahead, behind = lax.rem(me_g + 2, groups), lax.rem(me_g + groups - 2, groups)
    across = lax.rem(me_g + 4, groups)
    steps = head // block
    later = tail_ref.shape[0] // block
    tiles, width = qt_ref.shape[0], qt_ref.shape[2]
    half = q_hbm.shape[0] // 2
    mine_q = qall_ref.at[me_g]

    cand_copy = pltpu.make_async_copy(cand_hbm, cand_ref, cand_sem)
    cand_copy.start()
    own = pltpu.make_async_copy(q_hbm, mine_q, own_sem)
    own.start()
    fetch = [
        pltpu.make_async_copy(
            cent_hbm.at[pl.ds(b * block, block)], head_buf.at[pl.ds(b * block, block)], csem.at[b]
        )
        for b in range(steps)
    ]
    fetch_tail = [
        pltpu.make_async_copy(
            cent_hbm.at[pl.ds(head + b * block, block)], tail_ref.at[pl.ds(b * block, block)], tsem.at[b]
        )
        for b in range(later)
    ]
    codes_copy = pltpu.make_async_copy(codes_hbm, codes_ref, codes_sem)
    words_copy = pltpu.make_async_copy(words_hbm, words_ref, wsem)
    cand_copy.wait()
    row_buf[me_c] = jnp.concatenate([cand_ref[0:1, :], cand_ref[1:2, :]], axis=1)
    greeted = greet((("cent", me_c, cents), ("grp", me_g, groups)))
    own.wait()
    fetch[0].start()
    codes_copy.start()
    for copy in fetch[1:] + fetch_tail:
        copy.start()
    words_copy.start()
    for t in range(tiles):
        qt_ref[t] = qall_ref[me_g, t * width : (t + 1) * width, :].T
    acc_ref[...] = jnp.full(acc_ref.shape, -jnp.inf, jnp.float32)
    codes_copy.wait()
    by_token = codes_ref[...].T
    for part in range(codes_ref.shape[1] // 32):
        span = slice(part * pass_dev, (part + 1) * pass_dev)
        picks_ref[:, span] = by_token[part * 32 : (part + 1) * 32, :]
    greeted()

    gather_rows = [
        push(row_buf.at[me_c], row_buf.at[me_c], s1.at[d], r1.at[d], "cent", lax.rem(me_c + d, cents))
        for d in range(1, cents)
    ]
    gather_groups = [
        push(row_buf, all_buf.at[me_g], s2.at[d], r2.at[d], "grp", lax.rem(me_g + d, groups))
        for d in range(1, groups)
    ]

    low, high = pl.ds(0, half), pl.ds(half, half)
    lanes = iter(range(sq.shape[0]))

    def hand(block_of, span, peer):
        k = next(lanes)
        held = qall_ref.at[block_of, span]
        return push(held, held, sq.at[k], rq.at[k], "grp", peer)

    ahead_low, behind_high = hand(me_g, low, ahead), hand(me_g, high, behind)
    ahead_high, behind_low = hand(me_g, high, ahead), hand(me_g, low, behind)
    to_partner = hand(me_g, pl.ds(0, 2 * half), partner)
    relay_ahead, relay_behind = hand(behind, low, ahead), hand(ahead, high, behind)
    shares = [
        hand(block_of, span, partner)
        for block_of, span in (
            (behind, low), (ahead, high), (behind, high), (ahead, low), (across, low), (across, high)
        )
    ]

    for copy in gather_rows:
        copy.start()
    for copy in (ahead_low, behind_high, ahead_high, behind_low, to_partner):
        copy.start()

    def step(b, _):
        here = pl.ds(pl.multiple_of(b * block, block), block)
        pltpu.make_async_copy(cent_hbm.at[here], head_buf.at[here], csem.at[b]).wait()

        @pl.when(b == 2)
        def _():
            for copy in gather_rows:
                copy.wait_recv()
            for copy in gather_groups:
                copy.start()

        @pl.when(b == 3)
        def _():
            ahead_low.wait_recv()
            relay_ahead.start()
            shares[0].start()
            behind_high.wait_recv()
            relay_behind.start()
            shares[1].start()

        @pl.when(b == 6)
        def _():
            ahead_high.wait_recv()
            shares[2].start()
            behind_low.wait_recv()
            shares[3].start()

        table_ref[here, :] = head_buf[here, :].astype(jnp.float32)
        for t in range(tiles):
            scores = jnp.dot(head_buf[here, :], qt_ref[t], preferred_element_type=jnp.float32)
            top = jnp.max(scores.reshape(block // 8, 8, width), axis=0)
            acc_ref[t] = jnp.maximum(acc_ref[t], top)
        return 0

    lax.fori_loop(0, steps, step, 0)
    for copy in fetch_tail:
        copy.wait()
    part_rows = 1024

    def widen(r, _):
        src = pl.ds(pl.multiple_of(r * part_rows, part_rows), part_rows)
        dst = pl.ds(pl.multiple_of(head + r * part_rows, part_rows), part_rows)
        table_ref[dst, :] = tail_ref[src, :].astype(jnp.float32)
        return 0

    lax.fori_loop(0, tail_ref.shape[0] // part_rows, widen, 0)

    relay_ahead.wait_recv()
    shares[4].start()
    relay_behind.wait_recv()
    shares[5].start()
    for copy in gather_groups:
        copy.wait_recv()
    all_buf[me_g] = row_buf[...]
    for g in range(groups):
        for c in range(cents):
            rows[pl.ds(g * cents + c, 1), :] = all_buf[g, c]
    found = rows[...]
    lane = lax.broadcasted_iota(jnp.int32, found.shape, 1)
    mine = jnp.right_shift(found, pass_dev.bit_length() - 1) == me_c * groups + me_g
    packed = (lane * pass_dev + jnp.bitwise_and(found, pass_dev - 1)).astype(jnp.float32)
    first = jnp.min(jnp.where(mine, packed, float(EMPTY)), axis=1, keepdims=True)
    last = jnp.max(jnp.where(mine, packed, -1.0), axis=1, keepdims=True)
    ends = jnp.where(lane == 0, first, jnp.where(lane == 1, last, 0.0))
    ends_ref[...] = ends
    turned = ends.T[0:8, :].astype(jnp.int32)
    source = lax.broadcasted_iota(jnp.int32, turned.shape, 1)
    slot = lax.broadcasted_iota(jnp.int32, turned.shape, 0)
    other = jnp.where(slot == 1, jnp.broadcast_to(turned[0:1, :], turned.shape), -1)
    there = (turned < EMPTY) & (turned > other)
    query = 2 * source + jnp.right_shift(turned, (pass_dev * cand_count).bit_length() - 1)
    entry = jnp.bitwise_and(turned, pass_dev - 1) + pass_dev * (
        query + 2 * cents * groups * (slot * cents * groups + source)
    )
    entry_ref[...] = jnp.where(there, entry, -1)

    words_copy.wait()
    for copy in gather_rows + gather_groups:
        copy.wait_send()
    for copy in (ahead_low, behind_high, ahead_high, behind_low, relay_ahead, relay_behind):
        copy.wait_send()
    for copy in [to_partner] + shares:
        copy.wait()


def passage_kernel(
    cents, groups, pass_dev, plen, qtok, opening,
    entries, len_ref, ends_ref, lev_ref, picks_ref, table, tail, words, q_ref, qt_ref, acc_in,
    out_ref, best_ref,
    items, starts, units, seen, dense, embeds, totals, acc, spread, csem, *picks,
):
    srcs = groups * cents
    tiles = qt_ref.shape[0]
    rows_of_piece = PIECE
    pieces = tail.shape[0] // rows_of_piece * tiles
    loads = [
        pltpu.make_async_copy(picks_ref.at[r], picks[r], csem.at[r]) for r in range(len(picks))
    ]
    for copy in loads:
        copy.start()
    acc[...] = acc_in[...]

    def piece(m):
        t = lax.rem(m, tiles)
        start = pl.multiple_of(m // tiles * rows_of_piece, rows_of_piece)
        scores = jnp.dot(
            tail[pl.ds(start, rows_of_piece), :], qt_ref[t], preferred_element_type=jnp.float32
        )
        top = jnp.max(scores.reshape(rows_of_piece // 8, 8, scores.shape[1]), axis=0)
        acc[t] = jnp.maximum(acc[t], top)

    def collect(src, state):
        count, used = state
        pair = [entries[slot * srcs + src] for slot in range(2)]
        there = [entry >= 0 for entry in pair]
        owned = [jnp.bitwise_and(entry, pass_dev - 1) for entry in pair]
        marks = [jnp.where(ok, passage, pass_dev) for ok, passage in zip(there, owned)]
        known = [seen[mark] for mark in marks]
        sizes = [jnp.right_shift(len_ref[passage] + 31, 5) for passage in owned]
        for n in range(2):
            at = jnp.where(known[n] < 0, used, known[n])
            items[count] = pair[n]
            starts[count] = at
            seen[marks[n]] = at
            for part in range(plen // 32):
                units[used + part] = owned[n] + part * pass_dev
            count = count + jnp.where(there[n], 1, 0)
            used = used + jnp.where(there[n] & (known[n] < 0), sizes[n], 0)
        return count, used

    def open_step(m, state):
        piece(m)
        for k in range(srcs // opening):
            state = collect(m * (srcs // opening) + k, state)
        return state

    for k in range(len(spread)):
        spread[k][...] = jnp.zeros(spread[k].shape, spread[k].dtype)
    def forget(k, _):
        seen[k] = -1
        return 0

    seen[pass_dev] = 0
    lax.fori_loop(0, pass_dev, forget, 0, unroll=16)
    count, used = lax.fori_loop(0, opening, open_step, (jnp.int32(0), jnp.int32(0)))
    for pad in range(BATCH):
        items[count + pad] = 2 * srcs * (2 * srcs) * pass_dev
        starts[count + pad] = 0
    for pad in range(UNITS):
        units[used + pad] = 0
    totals[...] = jnp.zeros(totals.shape, jnp.float32)
    for copy in loads:
        copy.wait()

    sub = lax.broadcasted_iota(jnp.int32, (8, 128), 0)
    level = [jnp.broadcast_to(lev_ref[k : k + 1, :], (8, 128)) for k in range(4)]

    def embed(at):
        passage = jnp.bitwise_and(at, pass_dev - 1)
        part = jnp.right_shift(at, pass_dev.bit_length() - 1)
        word = words[passage, pl.ds(pl.multiple_of(part * 8, 8), 8), :]
        tiles = []
        for j in range(4):
            rows = None
            for s in range(8):
                row = table[pl.ds(picks[4 * s + j][at], 1), :]
                row = jnp.broadcast_to(row, (8, 128))
                rows = row if rows is None else jnp.where(sub == s, row, rows)
            low = jnp.bitwise_and(word, 1 << (2 * j)) != 0
            high = jnp.bitwise_and(word, 2 << (2 * j)) != 0
            residual = jnp.where(
                high, jnp.where(low, level[3], level[2]), jnp.where(low, level[1], level[0])
            )
            tiles.append(rows + residual)
        return tiles

    def finish(turn):
        for k in range(UNITS):
            tiles = []
            for j in range(4):
                value = dense[k * 32 + j * 8 : k * 32 + j * 8 + 8, :]
                squares = jnp.sum(value * value, axis=1, keepdims=True)
                tiles.append(value * lax.rsqrt(squares + 1e-06))
            at = pl.multiple_of(turn * (UNITS * 32) + k * 32, 32)
            embeds[pl.ds(at, 32), :] = jnp.concatenate(tiles, axis=0).astype(jnp.bfloat16)

    def embed_step(i, _):
        finish(i)
        for k in range(UNITS):
            for j, tile in enumerate(embed(units[i * UNITS + k])):
                dense[k * 32 + j * 8 : k * 32 + j * 8 + 8, :] = tile
        return 0

    def piece_step(m, _):
        piece(m)
        return 0

    def both_step(i, _):
        piece(opening + i)
        return embed_step(i, 0)

    turns = pl.cdiv(used, UNITS)
    shared = jnp.minimum(turns, pieces - opening)
    lax.fori_loop(0, shared, both_step, 0)
    lax.fori_loop(shared, turns, embed_step, 0)
    lax.fori_loop(opening + shared, pieces, piece_step, 0)
    finish(turns)
    embeds[pl.ds(pl.multiple_of((turns + 1) * (UNITS * 32), 32), plen), :] = jnp.zeros(
        (plen, embeds.shape[1]), embeds.dtype
    )
    for t in range(tiles):
        width = acc.shape[2]
        best_ref[:, t * width : (t + 1) * width] = jnp.max(acc[t], axis=0, keepdims=True)

    lane_q = lax.broadcasted_iota(jnp.int32, (8, 128), 1)
    four = 128 // qtok

    def score_step(batch, _):
        for k, wide in enumerate(spread):
            limit, rows, held = None, [], []
            for n in range(four):
                i = batch * BATCH + k * four + n
                entry = items[i]
                query = jnp.bitwise_and(jnp.right_shift(entry, pass_dev.bit_length() - 1), 2 * srcs - 1)
                rows.append(jnp.right_shift(entry, (2 * srcs * pass_dev).bit_length() - 1))
                length = len_ref[jnp.bitwise_and(entry, pass_dev - 1)]
                wide[n * qtok : (n + 1) * qtok, n * 128 : (n + 1) * 128] = q_ref[query]
                limit = length if limit is None else jnp.where(lane_q >= n * qtok, length, limit)
                held.append(embeds[pl.ds(pl.multiple_of((starts[i] + UNITS) * 32, 32), plen), :])
            scores = lax.dot_general(
                jnp.concatenate(held, axis=1), wide[...], (((1,), (1,)), ((), ())), preferred_element_type=jnp.float32
            )
            top = None
            for part in range(plen // 32):
                for j in range(4):
                    at = part * 32 + j * 8
                    inside = 4 * sub + (part * 32 + j) < limit
                    tile = jnp.where(inside, scores[at : at + 8], MASKED)
                    top = tile if top is None else jnp.maximum(top, tile)
            line = jnp.max(top, axis=0, keepdims=True)
            for n in range(four):
                own = (lane_q[0:1] >= n * qtok) & (lane_q[0:1] < (n + 1) * qtok)
                totals[pl.ds(rows[n], 1), :] = jnp.where(own, line, 0.0)
        return 0

    lax.fori_loop(0, pl.cdiv(count, BATCH), score_step, 0)

    value = jnp.sum(totals[0 : 2 * srcs, :], axis=1, keepdims=True) * (1.0 / qtok)
    ends = ends_ref[...]
    lane = lax.broadcasted_iota(jnp.int32, (srcs, srcs), 1)
    place = jnp.right_shift(ends.astype(jnp.int32), pass_dev.bit_length() - 1)
    low, high = place[:, 0:1], place[:, 1:2]
    second = ends[:, 1:2] > ends[:, 0:1]
    out_ref[...] = jnp.where(lane == low, value[0:srcs], 0.0) + jnp.where(
        (lane == high) & second, value[srcs : 2 * srcs], 0.0
    )


def return_kernel(
    cents, groups,
    best_ref, part_ref,
    token_ref, score_ref,
    best_buf, part_buf, sum_buf, row_buf, sb, rb, s1, r1, s2, r2,
):
    me_c, me_g = lax.axis_index("cent"), lax.axis_index("grp")
    greet((("cent", me_c, cents), ("grp", me_g, groups)))()

    def rows_of(g):
        return part_ref.at[pl.ds(pl.multiple_of(g * cents, cents), cents)]

    blocks, tops, lines = [], [], []
    for d in range(1, groups):
        peer = lax.rem(me_g + d, groups)
        blocks.append(push(rows_of(peer), part_buf.at[me_g], s1.at[d], r1.at[d], "grp", peer))
    for d in range(1, cents):
        peer = lax.rem(me_c + d, cents)
        tops.append(push(best_ref, best_buf.at[me_c], sb.at[d], rb.at[d], "cent", peer))
        lines.append(push(sum_buf.at[peer], row_buf.at[me_c], s2.at[d], r2.at[d], "cent", peer))
    for copy in blocks:
        copy.start()
    for copy in tops:
        copy.start()
    part_buf[me_g] = part_ref[pl.ds(pl.multiple_of(me_g * cents, cents), cents), :]
    best_buf[me_c] = best_ref[...]
    for copy in blocks:
        copy.wait_recv()
    total = part_buf[0]
    for g in range(1, groups):
        total = total + part_buf[g]
    for c in range(cents):
        sum_buf[c] = total[c : c + 1, :]
    row_buf[me_c] = sum_buf[me_c]
    for copy in lines:
        copy.start()

    for copy in tops:
        copy.wait_recv()
    top = best_buf[0]
    for c in range(1, cents):
        top = jnp.maximum(top, best_buf[c])
    width = token_ref.shape[1]
    for r in range(token_ref.shape[0]):
        token_ref[r : r + 1, :] = top[:, r * width : (r + 1) * width]

    for copy in lines:
        copy.wait_recv()
    line = row_buf[0]
    for c in range(1, cents):
        line = line + row_buf[c]
    half = score_ref.shape[1]
    score_ref[0:1, :] = line[:, 0:half]
    score_ref[1:2, :] = line[:, half : 2 * half]
    for copy in blocks + tops + lines:
        copy.wait_send()


def shards(queries, centroids, candidates, token_codes, resid_words, lengths, levels):
    query_rows, qtok, width = queries.shape
    cent_dev = centroids.shape[0]
    pass_dev, plen = token_codes.shape
    packed = resid_words.shape[1]
    per_device, cand_count = candidates.shape[2:]
    cents, groups = lax.axis_size("cent"), lax.axis_size("grp")
    srcs = cents * groups
    tokens = query_rows * qtok
    block, head = 2048, cent_dev // 2
    tiles = tokens // 256
    mib = 1 << 20
    dma = pltpu.SemaphoreType.DMA
    f32, i32, bf16 = jnp.float32, jnp.int32, jnp.bfloat16
    sds = jax.ShapeDtypeStruct
    hbm = functools.partial(pltpu.with_memory_space_constraint, memory_space=pltpu.HBM)

    table, tail, words, qall, qt, acc, picks, ends, entries = pl.pallas_call(
        functools.partial(search_kernel, cents, groups, pass_dev, block, head, cand_count),
        out_shape=(
            sds((cent_dev, width), f32),
            sds((cent_dev - head, width), bf16),
            sds((pass_dev, packed, width), i32),
            sds((groups, tokens, width), bf16),
            sds((tiles, width, 256), bf16),
            sds((tiles, 8, 256), f32),
            sds((32, plen // 32 * pass_dev), i32),
            sds((srcs, srcs), f32),
            sds((8, srcs), i32),
        ),
        in_specs=[ANY] * 5,
        out_specs=(VMEM,) * 9,
        scratch_shapes=[
            pltpu.VMEM((per_device, cand_count), i32),
            pltpu.VMEM((pass_dev, plen), i32),
            pltpu.VMEM((head, width), bf16),
            pltpu.VMEM((cents, 1, srcs), i32),
            pltpu.VMEM((groups, cents, 1, srcs), i32),
            pltpu.VMEM((srcs, srcs), i32),
            dma((head // block,)),
            dma(((cent_dev - head) // block,)),
            dma,
            dma,
            dma,
            dma,
            dma((cents,)),
            dma((cents,)),
            dma((groups,)),
            dma((groups,)),
            dma((13,)),
            dma((13,)),
        ],
        compiler_params=pltpu.CompilerParams(
            collective_id=0, has_side_effects=True, vmem_limit_bytes=8 * mib
        ),
        name="search",
    )(
        hbm(queries.reshape(tokens, width)),
        hbm(candidates.reshape(per_device, cand_count)),
        hbm(token_codes),
        hbm(centroids),
        hbm(resid_words),
    )

    slots = 2 * srcs
    parts, best = pl.pallas_call(
        functools.partial(passage_kernel, cents, groups, pass_dev, plen, qtok, OPENING),
        out_shape=(sds((srcs, srcs), f32), sds((1, tokens), f32)),
        in_specs=[SMEM, SMEM, VMEM, VMEM, ANY, VMEM, VMEM, VMEM, VMEM, VMEM, VMEM],
        out_specs=(VMEM, VMEM),
        scratch_shapes=[
            pltpu.SMEM((slots + BATCH,), i32),
            pltpu.SMEM((slots + BATCH,), i32),
            pltpu.SMEM((slots * (plen // 32) + UNITS + 4,), i32),
            pltpu.SMEM((pass_dev + 1,), i32),
            pltpu.VMEM((UNITS * 32, width), f32),
            pltpu.VMEM((slots * plen + 2 * UNITS * 32 + plen, width), bf16),
            pltpu.VMEM((slots + 8, 128), f32),
            pltpu.VMEM((tiles, 8, 256), f32),
            [pltpu.VMEM((128, 128 // qtok * width), bf16) for _ in range(BATCH * qtok // 128)],
            dma((32,)),
            *[pltpu.SMEM((plen // 32 * pass_dev,), i32) for _ in range(32)],
        ],
        compiler_params=pltpu.CompilerParams(vmem_limit_bytes=14 * mib),
        name="passages",
    )(
        entries.reshape(8 * srcs),
        lengths,
        ends,
        levels,
        picks,
        table,
        tail,
        words,
        qall.reshape(groups * query_rows, qtok, width),
        qt,
        acc,
    )

    token_best, scores = pl.pallas_call(
        functools.partial(return_kernel, cents, groups),
        out_shape=(sds((query_rows, qtok), f32), sds((per_device, cand_count), f32)),
        in_specs=[VMEM, VMEM],
        out_specs=(VMEM, VMEM),
        scratch_shapes=[
            pltpu.VMEM((cents, 1, tokens), f32),
            pltpu.VMEM((groups, cents, srcs), f32),
            pltpu.VMEM((cents, 1, srcs), f32),
            pltpu.VMEM((cents, 1, srcs), f32),
            dma((cents,)),
            dma((cents,)),
            dma((groups,)),
            dma((groups,)),
            dma((cents,)),
            dma((cents,)),
        ],
        compiler_params=pltpu.CompilerParams(
            collective_id=1, has_side_effects=True, vmem_limit_bytes=4 * mib
        ),
        name="returns",
    )(best, parts)
    return token_best, scores.reshape(1, 1, per_device, cand_count)


def solution(mesh):
    placed = (
        P("grp", None, None),
        P("cent", None),
        P("grp", "cent", None, None),
        P(("cent", "grp"), None),
        P(("cent", "grp"), None, None),
        P(("cent", "grp")),
        P(),
    )
    return jax.shard_map(
        shards,
        mesh=mesh,
        in_specs=placed,
        out_specs=(P("grp", None), P("grp", "cent", None, None)),
        check_vma=False,
    )
```

```python
import functools

import jax
import jax.numpy as jnp
from jax import lax
from jax.experimental import pallas as pl
from jax.experimental.pallas import tpu as pltpu
from jax.sharding import PartitionSpec as P

MESH = pl.DeviceIdType.MESH
ANY = pl.BlockSpec(memory_space=pl.ANY)
VMEM = pl.BlockSpec(memory_space=pltpu.VMEM)
SMEM = pl.BlockSpec(memory_space=pltpu.SMEM)
EMPTY = 1 << 20
MASKED = -1000000000.0
UNITS = 8
BATCH = 32
PIECE = 1024
OPENING = 8


def greet(axis_peers):
    barrier = pltpu.get_barrier_semaphore()
    total = 0
    for axis, me, size in axis_peers:
        for d in range(1, size):
            pl.semaphore_signal(
                barrier, inc=1, device_id={axis: lax.rem(me + d, size)}, device_id_type=MESH
            )
            total += 1
    return lambda: pl.semaphore_wait(barrier, total)


def push(src, dst, send, recv, axis, peer):
    return pltpu.make_async_remote_copy(
        src_ref=src,
        dst_ref=dst,
        send_sem=send,
        recv_sem=recv,
        device_id={axis: peer},
        device_id_type=MESH,
    )


def search_kernel(
    cents, groups, pass_dev, block, head, cand_count,
    q_hbm, cand_hbm, codes_hbm, cent_hbm, words_hbm,
    table_ref, tail_ref, words_ref, qall_ref, qt_ref, acc_ref, picks_ref, ends_ref, entry_ref,
    cand_ref, codes_ref, head_buf, row_buf, all_buf, rows, csem, tsem, wsem, own_sem, cand_sem, codes_sem, s1, r1, s2, r2, sq, rq,
):
    me_c, me_g = lax.axis_index("cent"), lax.axis_index("grp")
    partner = me_g + 1 - 2 * lax.rem(me_g, 2)
    ahead, behind = lax.rem(me_g + 2, groups), lax.rem(me_g + groups - 2, groups)
    across = lax.rem(me_g + 4, groups)
    steps = head // block
    later = tail_ref.shape[0] // block
    tiles, width = qt_ref.shape[0], qt_ref.shape[2]
    half = q_hbm.shape[0] // 2
    mine_q = qall_ref.at[me_g]

    cand_copy = pltpu.make_async_copy(cand_hbm, cand_ref, cand_sem)
    cand_copy.start()
    own = pltpu.make_async_copy(q_hbm, mine_q, own_sem)
    own.start()
    fetch = [
        pltpu.make_async_copy(
            cent_hbm.at[pl.ds(b * block, block)], head_buf.at[pl.ds(b * block, block)], csem.at[b]
        )
        for b in range(steps)
    ]
    fetch_tail = [
        pltpu.make_async_copy(
            cent_hbm.at[pl.ds(head + b * block, block)], tail_ref.at[pl.ds(b * block, block)], tsem.at[b]
        )
        for b in range(later)
    ]
    codes_copy = pltpu.make_async_copy(codes_hbm, codes_ref, codes_sem)
    words_copy = pltpu.make_async_copy(words_hbm, words_ref, wsem)
    cand_copy.wait()
    row_buf[me_c] = jnp.concatenate([cand_ref[0:1, :], cand_ref[1:2, :]], axis=1)
    greeted = greet((("cent", me_c, cents), ("grp", me_g, groups)))
    own.wait()
    fetch[0].start()
    codes_copy.start()
    for copy in fetch[1:] + fetch_tail:
        copy.start()
    words_copy.start()
    for t in range(tiles):
        qt_ref[t] = qall_ref[me_g, t * width : (t + 1) * width, :].T
    acc_ref[...] = jnp.full(acc_ref.shape, -jnp.inf, jnp.float32)
    codes_copy.wait()
    by_token = codes_ref[...].T
    for part in range(codes_ref.shape[1] // 32):
        span = slice(part * pass_dev, (part + 1) * pass_dev)
        picks_ref[:, span] = by_token[part * 32 : (part + 1) * 32, :]
    greeted()

    gather_rows = [
        push(row_buf.at[me_c], row_buf.at[me_c], s1.at[d], r1.at[d], "cent", lax.rem(me_c + d, cents))
        for d in range(1, cents)
    ]
    gather_groups = [
        push(row_buf, all_buf.at[me_g], s2.at[d], r2.at[d], "grp", lax.rem(me_g + d, groups))
        for d in range(1, groups)
    ]

    low, high = pl.ds(0, half), pl.ds(half, half)
    lanes = iter(range(sq.shape[0]))

    def hand(block_of, span, peer):
        k = next(lanes)
        held = qall_ref.at[block_of, span]
        return push(held, held, sq.at[k], rq.at[k], "grp", peer)

    ahead_low, behind_high = hand(me_g, low, ahead), hand(me_g, high, behind)
    ahead_high, behind_low = hand(me_g, high, ahead), hand(me_g, low, behind)
    to_partner = hand(me_g, pl.ds(0, 2 * half), partner)
    relay_ahead, relay_behind = hand(behind, low, ahead), hand(ahead, high, behind)
    shares = [
        hand(block_of, span, partner)
        for block_of, span in (
            (behind, low), (ahead, high), (behind, high), (ahead, low), (across, low), (across, high)
        )
    ]

    for copy in gather_rows:
        copy.start()
    for copy in (ahead_low, behind_high, ahead_high, behind_low, to_partner):
        copy.start()

    def step(b, _):
        here = pl.ds(pl.multiple_of(b * block, block), block)
        pltpu.make_async_copy(cent_hbm.at[here], head_buf.at[here], csem.at[b]).wait()

        @pl.when(b == 4)
        def _():
            for copy in gather_rows:
                copy.wait_recv()
            for copy in gather_groups:
                copy.start()

        @pl.when(b == 3)
        def _():
            ahead_low.wait_recv()
            relay_ahead.start()
            shares[0].start()
            behind_high.wait_recv()
            relay_behind.start()
            shares[1].start()

        @pl.when(b == 5)
        def _():
            ahead_high.wait_recv()
            shares[2].start()
            behind_low.wait_recv()
            shares[3].start()

        @pl.when(b == 7)
        def _():
            relay_ahead.wait_recv()
            shares[4].start()
            relay_behind.wait_recv()
            shares[5].start()

        beyond = pl.ds(pl.multiple_of(head + b * block, block), block)
        pltpu.make_async_copy(cent_hbm.at[beyond], tail_ref.at[here], tsem.at[b]).wait()
        table_ref[beyond, :] = tail_ref[here, :].astype(jnp.float32)
        table_ref[here, :] = head_buf[here, :].astype(jnp.float32)
        for t in range(tiles):
            scores = jnp.dot(head_buf[here, :], qt_ref[t], preferred_element_type=jnp.float32)
            top = jnp.max(scores.reshape(block // 8, 8, width), axis=0)
            acc_ref[t] = jnp.maximum(acc_ref[t], top)
        return 0

    lax.fori_loop(0, steps, step, 0)
    for copy in gather_groups:
        copy.wait_recv()
    all_buf[me_g] = row_buf[...]
    for g in range(groups):
        for c in range(cents):
            rows[pl.ds(g * cents + c, 1), :] = all_buf[g, c]
    found = rows[...]
    lane = lax.broadcasted_iota(jnp.int32, found.shape, 1)
    mine = jnp.right_shift(found, pass_dev.bit_length() - 1) == me_c * groups + me_g
    packed = (lane * pass_dev + jnp.bitwise_and(found, pass_dev - 1)).astype(jnp.float32)
    first = jnp.min(jnp.where(mine, packed, float(EMPTY)), axis=1, keepdims=True)
    last = jnp.max(jnp.where(mine, packed, -1.0), axis=1, keepdims=True)
    ends = jnp.where(lane == 0, first, jnp.where(lane == 1, last, 0.0))
    ends_ref[...] = ends
    turned = ends.T[0:8, :].astype(jnp.int32)
    source = lax.broadcasted_iota(jnp.int32, turned.shape, 1)
    slot = lax.broadcasted_iota(jnp.int32, turned.shape, 0)
    other = jnp.where(slot == 1, jnp.broadcast_to(turned[0:1, :], turned.shape), -1)
    there = (turned < EMPTY) & (turned > other)
    query = 2 * source + jnp.right_shift(turned, (pass_dev * cand_count).bit_length() - 1)
    entry = jnp.bitwise_and(turned, pass_dev - 1) + pass_dev * (
        query + 2 * cents * groups * (slot * cents * groups + source)
    )
    entry_ref[...] = jnp.where(there, entry, -1)

    words_copy.wait()
    for copy in gather_rows + gather_groups:
        copy.wait_send()
    for copy in (ahead_low, behind_high, ahead_high, behind_low, relay_ahead, relay_behind):
        copy.wait_send()
    for copy in [to_partner] + shares:
        copy.wait()


def passage_kernel(
    cents, groups, pass_dev, plen, qtok, opening,
    entries, len_ref, ends_ref, lev_ref, picks_ref, table, tail, words, q_ref, qt_ref, acc_in,
    out_ref, best_ref,
    items, starts, units, seen, dense, embeds, totals, acc, spread, csem, *picks,
):
    srcs = groups * cents
    tiles = qt_ref.shape[0]
    rows_of_piece = PIECE
    pieces = tail.shape[0] // rows_of_piece * tiles
    loads = [
        pltpu.make_async_copy(picks_ref.at[r], picks[r], csem.at[r]) for r in range(len(picks))
    ]
    for copy in loads:
        copy.start()
    acc[...] = acc_in[...]

    def piece(m):
        t = lax.rem(m, tiles)
        start = pl.multiple_of(m // tiles * rows_of_piece, rows_of_piece)
        scores = jnp.dot(
            tail[pl.ds(start, rows_of_piece), :], qt_ref[t], preferred_element_type=jnp.float32
        )
        top = jnp.max(scores.reshape(rows_of_piece // 8, 8, scores.shape[1]), axis=0)
        acc[t] = jnp.maximum(acc[t], top)

    def collect(src, state):
        count, used = state
        pair = [entries[slot * srcs + src] for slot in range(2)]
        there = [entry >= 0 for entry in pair]
        owned = [jnp.bitwise_and(entry, pass_dev - 1) for entry in pair]
        marks = [jnp.where(ok, passage, pass_dev) for ok, passage in zip(there, owned)]
        known = [seen[mark] for mark in marks]
        sizes = [jnp.right_shift(len_ref[passage] + 31, 5) for passage in owned]
        for n in range(2):
            at = jnp.where(known[n] < 0, used, known[n])
            items[count] = pair[n]
            starts[count] = at
            seen[marks[n]] = at
            for part in range(plen // 32):
                units[used + part] = owned[n] + part * pass_dev
            count = count + jnp.where(there[n], 1, 0)
            used = used + jnp.where(there[n] & (known[n] < 0), sizes[n], 0)
        return count, used

    def open_step(m, state):
        piece(m)
        for k in range(srcs // opening):
            state = collect(m * (srcs // opening) + k, state)
        return state

    for k in range(len(spread)):
        spread[k][...] = jnp.zeros(spread[k].shape, spread[k].dtype)
    def forget(k, _):
        seen[k] = -1
        return 0

    seen[pass_dev] = 0
    lax.fori_loop(0, pass_dev, forget, 0, unroll=16)
    count, used = lax.fori_loop(0, opening, open_step, (jnp.int32(0), jnp.int32(0)))
    for pad in range(BATCH):
        items[count + pad] = 2 * srcs * (2 * srcs) * pass_dev
        starts[count + pad] = 0
    for pad in range(UNITS):
        units[used + pad] = 0
    totals[...] = jnp.zeros(totals.shape, jnp.float32)
    for copy in loads:
        copy.wait()

    sub = lax.broadcasted_iota(jnp.int32, (8, 128), 0)
    level = [jnp.broadcast_to(lev_ref[k : k + 1, :], (8, 128)) for k in range(4)]

    def embed(at):
        passage = jnp.bitwise_and(at, pass_dev - 1)
        part = jnp.right_shift(at, pass_dev.bit_length() - 1)
        word = words[passage, pl.ds(pl.multiple_of(part * 8, 8), 8), :]
        tiles = []
        for j in range(4):
            rows = None
            for s in range(8):
                row = table[pl.ds(picks[4 * s + j][at], 1), :]
                row = jnp.broadcast_to(row, (8, 128))
                rows = row if rows is None else jnp.where(sub == s, row, rows)
            low = jnp.bitwise_and(word, 1 << (2 * j)) != 0
            high = jnp.bitwise_and(word, 2 << (2 * j)) != 0
            residual = jnp.where(
                high, jnp.where(low, level[3], level[2]), jnp.where(low, level[1], level[0])
            )
            tiles.append(rows + residual)
        return tiles

    def finish(turn):
        for k in range(UNITS):
            tiles = []
            for j in range(4):
                value = dense[k * 32 + j * 8 : k * 32 + j * 8 + 8, :]
                squares = jnp.sum(value * value, axis=1, keepdims=True)
                tiles.append(value * lax.rsqrt(squares + 1e-06))
            at = pl.multiple_of(turn * (UNITS * 32) + k * 32, 32)
            embeds[pl.ds(at, 32), :] = jnp.concatenate(tiles, axis=0).astype(jnp.bfloat16)

    def embed_step(i, _):
        finish(i)
        for k in range(UNITS):
            for j, tile in enumerate(embed(units[i * UNITS + k])):
                dense[k * 32 + j * 8 : k * 32 + j * 8 + 8, :] = tile
        return 0

    def piece_step(m, _):
        piece(m)
        return 0

    def both_step(i, _):
        piece(opening + i)
        return embed_step(i, 0)

    turns = pl.cdiv(used, UNITS)
    shared = jnp.minimum(turns, pieces - opening)
    lax.fori_loop(0, shared, both_step, 0)
    lax.fori_loop(shared, turns, embed_step, 0)
    lax.fori_loop(opening + shared, pieces, piece_step, 0)
    finish(turns)
    embeds[pl.ds(pl.multiple_of((turns + 1) * (UNITS * 32), 32), plen), :] = jnp.zeros(
        (plen, embeds.shape[1]), embeds.dtype
    )
    for t in range(tiles):
        width = acc.shape[2]
        best_ref[:, t * width : (t + 1) * width] = jnp.max(acc[t], axis=0, keepdims=True)

    lane_q = lax.broadcasted_iota(jnp.int32, (8, 128), 1)
    four = 128 // qtok

    def score_step(batch, _):
        for k, wide in enumerate(spread):
            limit, rows, held = None, [], []
            for n in range(four):
                i = batch * BATCH + k * four + n
                entry = items[i]
                query = jnp.bitwise_and(jnp.right_shift(entry, pass_dev.bit_length() - 1), 2 * srcs - 1)
                rows.append(jnp.right_shift(entry, (2 * srcs * pass_dev).bit_length() - 1))
                length = len_ref[jnp.bitwise_and(entry, pass_dev - 1)]
                wide[n * qtok : (n + 1) * qtok, n * 128 : (n + 1) * 128] = q_ref[query]
                limit = length if limit is None else jnp.where(lane_q >= n * qtok, length, limit)
                held.append(embeds[pl.ds(pl.multiple_of((starts[i] + UNITS) * 32, 32), plen), :])
            scores = lax.dot_general(
                jnp.concatenate(held, axis=1), wide[...], (((1,), (1,)), ((), ())), preferred_element_type=jnp.float32
            )
            top = None
            for part in range(plen // 32):
                for j in range(4):
                    at = part * 32 + j * 8
                    inside = 4 * sub + (part * 32 + j) < limit
                    tile = jnp.where(inside, scores[at : at + 8], MASKED)
                    top = tile if top is None else jnp.maximum(top, tile)
            line = jnp.max(top, axis=0, keepdims=True)
            for n in range(four):
                own = (lane_q[0:1] >= n * qtok) & (lane_q[0:1] < (n + 1) * qtok)
                totals[pl.ds(rows[n], 1), :] = jnp.where(own, line, 0.0)
        return 0

    lax.fori_loop(0, pl.cdiv(count, BATCH), score_step, 0)

    value = jnp.sum(totals[0 : 2 * srcs, :], axis=1, keepdims=True) * (1.0 / qtok)
    ends = ends_ref[...]
    lane = lax.broadcasted_iota(jnp.int32, (srcs, srcs), 1)
    place = jnp.right_shift(ends.astype(jnp.int32), pass_dev.bit_length() - 1)
    low, high = place[:, 0:1], place[:, 1:2]
    second = ends[:, 1:2] > ends[:, 0:1]
    out_ref[...] = jnp.where(lane == low, value[0:srcs], 0.0) + jnp.where(
        (lane == high) & second, value[srcs : 2 * srcs], 0.0
    )


def return_kernel(
    cents, groups,
    best_ref, part_ref,
    token_ref, score_ref,
    best_buf, part_buf, sum_buf, row_buf, sb, rb, s1, r1, s2, r2,
):
    me_c, me_g = lax.axis_index("cent"), lax.axis_index("grp")
    greet((("cent", me_c, cents), ("grp", me_g, groups)))()

    def rows_of(g):
        return part_ref.at[pl.ds(pl.multiple_of(g * cents, cents), cents)]

    blocks, tops, lines = [], [], []
    for d in range(1, groups):
        peer = lax.rem(me_g + d, groups)
        blocks.append(push(rows_of(peer), part_buf.at[me_g], s1.at[d], r1.at[d], "grp", peer))
    for d in range(1, cents):
        peer = lax.rem(me_c + d, cents)
        tops.append(push(best_ref, best_buf.at[me_c], sb.at[d], rb.at[d], "cent", peer))
        lines.append(push(sum_buf.at[peer], row_buf.at[me_c], s2.at[d], r2.at[d], "cent", peer))
    for copy in blocks:
        copy.start()
    for copy in tops:
        copy.start()
    part_buf[me_g] = part_ref[pl.ds(pl.multiple_of(me_g * cents, cents), cents), :]
    best_buf[me_c] = best_ref[...]
    for copy in blocks:
        copy.wait_recv()
    total = part_buf[0]
    for g in range(1, groups):
        total = total + part_buf[g]
    for c in range(cents):
        sum_buf[c] = total[c : c + 1, :]
    row_buf[me_c] = sum_buf[me_c]
    for copy in lines:
        copy.start()

    for copy in tops:
        copy.wait_recv()
    top = best_buf[0]
    for c in range(1, cents):
        top = jnp.maximum(top, best_buf[c])
    width = token_ref.shape[1]
    for r in range(token_ref.shape[0]):
        token_ref[r : r + 1, :] = top[:, r * width : (r + 1) * width]

    for copy in lines:
        copy.wait_recv()
    line = row_buf[0]
    for c in range(1, cents):
        line = line + row_buf[c]
    half = score_ref.shape[1]
    score_ref[0:1, :] = line[:, 0:half]
    score_ref[1:2, :] = line[:, half : 2 * half]
    for copy in blocks + tops + lines:
        copy.wait_send()


def shards(queries, centroids, candidates, token_codes, resid_words, lengths, levels):
    query_rows, qtok, width = queries.shape
    cent_dev = centroids.shape[0]
    pass_dev, plen = token_codes.shape
    packed = resid_words.shape[1]
    per_device, cand_count = candidates.shape[2:]
    cents, groups = lax.axis_size("cent"), lax.axis_size("grp")
    srcs = cents * groups
    tokens = query_rows * qtok
    block, head = 2048, cent_dev // 2
    tiles = tokens // 256
    mib = 1 << 20
    dma = pltpu.SemaphoreType.DMA
    f32, i32, bf16 = jnp.float32, jnp.int32, jnp.bfloat16
    sds = jax.ShapeDtypeStruct
    hbm = functools.partial(pltpu.with_memory_space_constraint, memory_space=pltpu.HBM)

    table, tail, words, qall, qt, acc, picks, ends, entries = pl.pallas_call(
        functools.partial(search_kernel, cents, groups, pass_dev, block, head, cand_count),
        out_shape=(
            sds((cent_dev, width), f32),
            sds((cent_dev - head, width), bf16),
            sds((pass_dev, packed, width), i32),
            sds((groups, tokens, width), bf16),
            sds((tiles, width, 256), bf16),
            sds((tiles, 8, 256), f32),
            sds((32, plen // 32 * pass_dev), i32),
            sds((srcs, srcs), f32),
            sds((8, srcs), i32),
        ),
        in_specs=[ANY] * 5,
        out_specs=(VMEM,) * 9,
        scratch_shapes=[
            pltpu.VMEM((per_device, cand_count), i32),
            pltpu.VMEM((pass_dev, plen), i32),
            pltpu.VMEM((head, width), bf16),
            pltpu.VMEM((cents, 1, srcs), i32),
            pltpu.VMEM((groups, cents, 1, srcs), i32),
            pltpu.VMEM((srcs, srcs), i32),
            dma((head // block,)),
            dma(((cent_dev - head) // block,)),
            dma,
            dma,
            dma,
            dma,
            dma((cents,)),
            dma((cents,)),
            dma((groups,)),
            dma((groups,)),
            dma((13,)),
            dma((13,)),
        ],
        compiler_params=pltpu.CompilerParams(
            collective_id=0, has_side_effects=True, vmem_limit_bytes=8 * mib
        ),
        name="search",
    )(
        hbm(queries.reshape(tokens, width)),
        hbm(candidates.reshape(per_device, cand_count)),
        hbm(token_codes),
        hbm(centroids),
        hbm(resid_words),
    )

    slots = 2 * srcs
    parts, best = pl.pallas_call(
        functools.partial(passage_kernel, cents, groups, pass_dev, plen, qtok, OPENING),
        out_shape=(sds((srcs, srcs), f32), sds((1, tokens), f32)),
        in_specs=[SMEM, SMEM, VMEM, VMEM, ANY, VMEM, VMEM, VMEM, VMEM, VMEM, VMEM],
        out_specs=(VMEM, VMEM),
        scratch_shapes=[
            pltpu.SMEM((slots + BATCH,), i32),
            pltpu.SMEM((slots + BATCH,), i32),
            pltpu.SMEM((slots * (plen // 32) + UNITS + 4,), i32),
            pltpu.SMEM((pass_dev + 1,), i32),
            pltpu.VMEM((UNITS * 32, width), f32),
            pltpu.VMEM((slots * plen + 2 * UNITS * 32 + plen, width), bf16),
            pltpu.VMEM((slots + 8, 128), f32),
            pltpu.VMEM((tiles, 8, 256), f32),
            [pltpu.VMEM((128, 128 // qtok * width), bf16) for _ in range(BATCH * qtok // 128)],
            dma((32,)),
            *[pltpu.SMEM((plen // 32 * pass_dev,), i32) for _ in range(32)],
        ],
        compiler_params=pltpu.CompilerParams(vmem_limit_bytes=14 * mib),
        name="passages",
    )(
        entries.reshape(8 * srcs),
        lengths,
        ends,
        levels,
        picks,
        table,
        tail,
        words,
        qall.reshape(groups * query_rows, qtok, width),
        qt,
        acc,
    )

    token_best, scores = pl.pallas_call(
        functools.partial(return_kernel, cents, groups),
        out_shape=(sds((query_rows, qtok), f32), sds((per_device, cand_count), f32)),
        in_specs=[VMEM, VMEM],
        out_specs=(VMEM, VMEM),
        scratch_shapes=[
            pltpu.VMEM((cents, 1, tokens), f32),
            pltpu.VMEM((groups, cents, srcs), f32),
            pltpu.VMEM((cents, 1, srcs), f32),
            pltpu.VMEM((cents, 1, srcs), f32),
            dma((cents,)),
            dma((cents,)),
            dma((groups,)),
            dma((groups,)),
            dma((cents,)),
            dma((cents,)),
        ],
        compiler_params=pltpu.CompilerParams(
            collective_id=1, has_side_effects=True, vmem_limit_bytes=4 * mib
        ),
        name="returns",
    )(best, parts)
    return token_best, scores.reshape(1, 1, per_device, cand_count)


def solution(mesh):
    placed = (
        P("grp", None, None),
        P("cent", None),
        P("grp", "cent", None, None),
        P(("cent", "grp"), None),
        P(("cent", "grp"), None, None),
        P(("cent", "grp")),
        P(),
    )
    return jax.shard_map(
        shards,
        mesh=mesh,
        in_specs=placed,
        out_specs=(P("grp", None), P("grp", "cent", None, None)),
        check_vma=False,
    )
```

```python
import functools

import jax
import jax.numpy as jnp
from jax import lax
from jax.experimental import pallas as pl
from jax.experimental.pallas import tpu as pltpu
from jax.sharding import PartitionSpec as P

MESH = pl.DeviceIdType.MESH
ANY = pl.BlockSpec(memory_space=pl.ANY)
VMEM = pl.BlockSpec(memory_space=pltpu.VMEM)
SMEM = pl.BlockSpec(memory_space=pltpu.SMEM)
EMPTY = 1 << 20
MASKED = -1000000000.0
UNITS = 8
BATCH = 32
PIECE = 1024
OPENING = 8


def greet(axis_peers):
    barrier = pltpu.get_barrier_semaphore()
    total = 0
    for axis, me, size in axis_peers:
        for d in range(1, size):
            pl.semaphore_signal(
                barrier, inc=1, device_id={axis: lax.rem(me + d, size)}, device_id_type=MESH
            )
            total += 1
    return lambda: pl.semaphore_wait(barrier, total)


def push(src, dst, send, recv, axis, peer):
    return pltpu.make_async_remote_copy(
        src_ref=src,
        dst_ref=dst,
        send_sem=send,
        recv_sem=recv,
        device_id={axis: peer},
        device_id_type=MESH,
    )


def search_kernel(
    cents, groups, pass_dev, block, head, cand_count,
    q_hbm, cand_hbm, codes_hbm, cent_hbm, words_hbm,
    table_ref, tail_ref, words_ref, qall_ref, qt_ref, acc_ref, picks_ref, ends_ref, entry_ref,
    cand_ref, codes_ref, head_buf, row_buf, all_buf, rows, csem, tsem, wsem, own_sem, cand_sem, codes_sem, s1, r1, s2, r2, sq, rq,
):
    me_c, me_g = lax.axis_index("cent"), lax.axis_index("grp")
    partner = me_g + 1 - 2 * lax.rem(me_g, 2)
    ahead, behind = lax.rem(me_g + 2, groups), lax.rem(me_g + groups - 2, groups)
    across = lax.rem(me_g + 4, groups)
    steps = head // block
    later = tail_ref.shape[0] // block
    tiles, width = qt_ref.shape[0], qt_ref.shape[2]
    half = q_hbm.shape[0] // 2
    mine_q = qall_ref.at[me_g]

    cand_copy = pltpu.make_async_copy(cand_hbm, cand_ref, cand_sem)
    cand_copy.start()
    own = pltpu.make_async_copy(q_hbm, mine_q, own_sem)
    own.start()
    fetch = [
        pltpu.make_async_copy(
            cent_hbm.at[pl.ds(b * block, block)], head_buf.at[pl.ds(b * block, block)], csem.at[b]
        )
        for b in range(steps)
    ]
    fetch_tail = [
        pltpu.make_async_copy(
            cent_hbm.at[pl.ds(head + b * block, block)], tail_ref.at[pl.ds(b * block, block)], tsem.at[b]
        )
        for b in range(later)
    ]
    codes_copy = pltpu.make_async_copy(codes_hbm, codes_ref, codes_sem)
    words_copy = pltpu.make_async_copy(words_hbm, words_ref, wsem)
    cand_copy.wait()
    row_buf[me_c] = jnp.concatenate([cand_ref[0:1, :], cand_ref[1:2, :]], axis=1)
    greeted = greet((("cent", me_c, cents), ("grp", me_g, groups)))
    own.wait()
    fetch[0].start()
    codes_copy.start()
    for copy in fetch[1:] + fetch_tail:
        copy.start()
    words_copy.start()
    for t in range(tiles):
        qt_ref[t] = qall_ref[me_g, t * width : (t + 1) * width, :].T
    acc_ref[...] = jnp.full(acc_ref.shape, -jnp.inf, jnp.float32)
    codes_copy.wait()
    by_token = codes_ref[...].T
    for part in range(codes_ref.shape[1] // 32):
        span = slice(part * pass_dev, (part + 1) * pass_dev)
        picks_ref[:, span] = by_token[part * 32 : (part + 1) * 32, :]
    greeted()

    gather_rows = [
        push(row_buf.at[me_c], row_buf.at[me_c], s1.at[d], r1.at[d], "cent", lax.rem(me_c + d, cents))
        for d in range(1, cents)
    ]
    gather_groups = [
        push(row_buf, all_buf.at[me_g], s2.at[d], r2.at[d], "grp", lax.rem(me_g + d, groups))
        for d in range(1, groups)
    ]

    low, high = pl.ds(0, half), pl.ds(half, half)
    lanes = iter(range(sq.shape[0]))

    def hand(block_of, span, peer):
        k = next(lanes)
        held = qall_ref.at[block_of, span]
        return push(held, held, sq.at[k], rq.at[k], "grp", peer)

    ahead_low, behind_high = hand(me_g, low, ahead), hand(me_g, high, behind)
    ahead_high, behind_low = hand(me_g, high, ahead), hand(me_g, low, behind)
    to_partner = hand(me_g, pl.ds(0, 2 * half), partner)
    relay_ahead, relay_behind = hand(behind, low, ahead), hand(ahead, high, behind)
    shares = [
        hand(block_of, span, partner)
        for block_of, span in (
            (behind, low), (ahead, high), (behind, high), (ahead, low), (across, low), (across, high)
        )
    ]

    for copy in gather_rows:
        copy.start()
    for copy in (ahead_low, behind_high, ahead_high, behind_low, to_partner):
        copy.start()

    def step(b, _):
        here = pl.ds(pl.multiple_of(b * block, block), block)
        pltpu.make_async_copy(cent_hbm.at[here], head_buf.at[here], csem.at[b]).wait()

        @pl.when(b == 4)
        def _():
            for copy in gather_rows:
                copy.wait_recv()
            for copy in gather_groups:
                copy.start()

        @pl.when(b == 3)
        def _():
            ahead_low.wait_recv()
            relay_ahead.start()
            shares[0].start()
            behind_high.wait_recv()
            relay_behind.start()
            shares[1].start()

        @pl.when(b == 5)
        def _():
            ahead_high.wait_recv()
            shares[2].start()
            behind_low.wait_recv()
            shares[3].start()

        @pl.when(b == 7)
        def _():
            relay_ahead.wait_recv()
            shares[4].start()
            relay_behind.wait_recv()
            shares[5].start()

        beyond = pl.ds(pl.multiple_of(head + b * block, block), block)
        pltpu.make_async_copy(cent_hbm.at[beyond], tail_ref.at[here], tsem.at[b]).wait()
        table_ref[beyond, :] = tail_ref[here, :].astype(jnp.float32)
        table_ref[here, :] = head_buf[here, :].astype(jnp.float32)
        for t in range(tiles):
            scores = jnp.dot(head_buf[here, :], qt_ref[t], preferred_element_type=jnp.float32)
            top = jnp.max(scores.reshape(block // 8, 8, width), axis=0)
            acc_ref[t] = jnp.maximum(acc_ref[t], top)
        return 0

    lax.fori_loop(0, steps, step, 0)
    for copy in gather_groups:
        copy.wait_recv()
    all_buf[me_g] = row_buf[...]
    for g in range(groups):
        for c in range(cents):
            rows[pl.ds(g * cents + c, 1), :] = all_buf[g, c]
    found = rows[...]
    lane = lax.broadcasted_iota(jnp.int32, found.shape, 1)
    mine = jnp.right_shift(found, pass_dev.bit_length() - 1) == me_c * groups + me_g
    packed = (lane * pass_dev + jnp.bitwise_and(found, pass_dev - 1)).astype(jnp.float32)
    first = jnp.min(jnp.where(mine, packed, float(EMPTY)), axis=1, keepdims=True)
    last = jnp.max(jnp.where(mine, packed, -1.0), axis=1, keepdims=True)
    ends = jnp.where(lane == 0, first, jnp.where(lane == 1, last, 0.0))
    ends_ref[...] = ends
    turned = ends.T[0:8, :].astype(jnp.int32)
    source = lax.broadcasted_iota(jnp.int32, turned.shape, 1)
    slot = lax.broadcasted_iota(jnp.int32, turned.shape, 0)
    other = jnp.where(slot == 1, jnp.broadcast_to(turned[0:1, :], turned.shape), -1)
    there = (turned < EMPTY) & (turned > other)
    query = 2 * source + jnp.right_shift(turned, (pass_dev * cand_count).bit_length() - 1)
    entry = jnp.bitwise_and(turned, pass_dev - 1) + pass_dev * (
        query + 2 * cents * groups * (slot * cents * groups + source)
    )
    entry_ref[...] = jnp.where(there, entry, -1)

    words_copy.wait()
    for copy in gather_rows + gather_groups:
        copy.wait_send()
    for copy in (ahead_low, behind_high, ahead_high, behind_low, relay_ahead, relay_behind):
        copy.wait_send()
    for copy in [to_partner] + shares:
        copy.wait()


def passage_kernel(
    cents, groups, pass_dev, plen, opening,
    entries, len_ref, lev_ref, picks_ref, table, tail, words, qt_ref, acc_in,
    embeds, starts, best_ref,
    units, seen, dense, acc, csem, *picks,
):
    srcs = groups * cents
    tiles = qt_ref.shape[0]
    rows_of_piece = PIECE
    pieces = tail.shape[0] // rows_of_piece * tiles
    loads = [
        pltpu.make_async_copy(picks_ref.at[r], picks[r], csem.at[r]) for r in range(len(picks))
    ]
    for copy in loads:
        copy.start()
    acc[...] = acc_in[...]

    def piece(m):
        t = lax.rem(m, tiles)
        start = pl.multiple_of(m // tiles * rows_of_piece, rows_of_piece)
        scores = jnp.dot(
            tail[pl.ds(start, rows_of_piece), :], qt_ref[t], preferred_element_type=jnp.float32
        )
        top = jnp.max(scores.reshape(rows_of_piece // 8, 8, scores.shape[1]), axis=0)
        acc[t] = jnp.maximum(acc[t], top)

    def collect(src, used):
        pair = [entries[slot * srcs + src] for slot in range(2)]
        there = [entry >= 0 for entry in pair]
        owned = [jnp.bitwise_and(entry, pass_dev - 1) for entry in pair]
        marks = [jnp.where(ok, passage, pass_dev) for ok, passage in zip(there, owned)]
        known = [seen[mark] for mark in marks]
        sizes = [jnp.right_shift(len_ref[passage] + 31, 5) for passage in owned]
        for n in range(2):
            at = jnp.where(known[n] < 0, used, known[n])
            starts[n * srcs + src] = jnp.where(there[n], at, 0) + UNITS
            seen[marks[n]] = at
            for part in range(plen // 32):
                units[used + part] = owned[n] + part * pass_dev
            used = used + jnp.where(there[n] & (known[n] < 0), sizes[n], 0)
        return used

    def open_step(m, state):
        piece(m)
        for k in range(srcs // opening):
            state = collect(m * (srcs // opening) + k, state)
        return state

    def forget(k, _):
        seen[k] = -1
        return 0

    seen[pass_dev] = 0
    lax.fori_loop(0, pass_dev, forget, 0, unroll=16)
    used = lax.fori_loop(0, opening, open_step, jnp.int32(0))
    for pad in range(UNITS):
        units[used + pad] = 0
    for copy in loads:
        copy.wait()

    sub = lax.broadcasted_iota(jnp.int32, (8, 128), 0)
    level = [jnp.broadcast_to(lev_ref[k : k + 1, :], (8, 128)) for k in range(4)]

    def embed(at):
        passage = jnp.bitwise_and(at, pass_dev - 1)
        part = jnp.right_shift(at, pass_dev.bit_length() - 1)
        word = words[passage, pl.ds(pl.multiple_of(part * 8, 8), 8), :]
        tiles = []
        for j in range(4):
            rows = None
            for s in range(8):
                row = table[pl.ds(picks[4 * s + j][at], 1), :]
                row = jnp.broadcast_to(row, (8, 128))
                rows = row if rows is None else jnp.where(sub == s, row, rows)
            low = jnp.bitwise_and(word, 1 << (2 * j)) != 0
            high = jnp.bitwise_and(word, 2 << (2 * j)) != 0
            residual = jnp.where(
                high, jnp.where(low, level[3], level[2]), jnp.where(low, level[1], level[0])
            )
            tiles.append(rows + residual)
        return tiles

    def finish(turn):
        for k in range(UNITS):
            tiles = []
            for j in range(4):
                value = dense[k * 32 + j * 8 : k * 32 + j * 8 + 8, :]
                squares = jnp.sum(value * value, axis=1, keepdims=True)
                tiles.append(value * lax.rsqrt(squares + 1e-06))
            embeds[turn * UNITS + k] = jnp.concatenate(tiles, axis=0).astype(jnp.bfloat16)

    def embed_step(i, _):
        finish(i)
        for k in range(UNITS):
            for j, tile in enumerate(embed(units[i * UNITS + k])):
                dense[k * 32 + j * 8 : k * 32 + j * 8 + 8, :] = tile
        return 0

    def piece_step(m, _):
        piece(m)
        return 0

    def both_step(i, _):
        piece(opening + i)
        return embed_step(i, 0)

    turns = pl.cdiv(used, UNITS)
    shared = jnp.minimum(turns, pieces - opening)
    lax.fori_loop(0, shared, both_step, 0)
    lax.fori_loop(shared, turns, embed_step, 0)
    lax.fori_loop(opening + shared, pieces, piece_step, 0)
    finish(turns)
    for k in range(plen // 32):
        embeds[(turns + 1) * UNITS + k] = jnp.zeros(embeds.shape[1:], embeds.dtype)
    for t in range(tiles):
        width = acc.shape[2]
        best_ref[:, t * width : (t + 1) * width] = jnp.max(acc[t], axis=0, keepdims=True)


def return_kernel(
    cents, groups, pass_dev, plen, qtok,
    entries, len_ref, starts, ends_ref, embeds, q_ref, best_ref,
    token_ref, score_ref,
    part_ref, totals, spread, best_buf, part_buf, sum_buf, row_buf, sb, rb, s1, r1, s2, r2,
):
    me_c, me_g = lax.axis_index("cent"), lax.axis_index("grp")
    srcs = cents * groups
    greeted = greet((("cent", me_c, cents), ("grp", me_g, groups)))
    lane_q = lax.broadcasted_iota(jnp.int32, (8, 128), 1)
    four = 128 // qtok

    sub = lax.broadcasted_iota(jnp.int32, (8, 128), 0)
    for wide in spread:
        wide[...] = jnp.zeros(wide.shape, wide.dtype)

    def score_step(batch, _):
        for k, wide in enumerate(spread):
            limit, held = None, []
            for n in range(four):
                i = batch * BATCH + k * four + n
                entry = entries[i]
                query = jnp.bitwise_and(jnp.right_shift(entry, pass_dev.bit_length() - 1), 2 * srcs - 1)
                length = len_ref[jnp.bitwise_and(entry, pass_dev - 1)]
                wide[n * qtok : (n + 1) * qtok, n * 128 : (n + 1) * 128] = q_ref[query]
                limit = length if limit is None else jnp.where(lane_q >= n * qtok, length, limit)
                first = starts[i]
                held.append(
                    jnp.concatenate([embeds[first + part] for part in range(plen // 32)], axis=0)
                )
            scores = lax.dot_general(
                jnp.concatenate(held, axis=1), wide[...], (((1,), (1,)), ((), ())), preferred_element_type=jnp.float32
            )
            top = None
            for part in range(plen // 32):
                for j in range(4):
                    at = part * 32 + j * 8
                    inside = 4 * sub + (part * 32 + j) < limit
                    tile = jnp.where(inside, scores[at : at + 8], MASKED)
                    top = tile if top is None else jnp.maximum(top, tile)
            line = jnp.max(top, axis=0, keepdims=True)
            for n in range(four):
                own = (lane_q[0:1] >= n * qtok) & (lane_q[0:1] < (n + 1) * qtok)
                totals[pl.ds(batch * BATCH + k * four + n, 1), :] = jnp.where(own, line, 0.0)
        return 0

    lax.fori_loop(0, 2 * srcs // BATCH, score_step, 0)

    value = jnp.sum(totals[...], axis=1, keepdims=True) * (1.0 / qtok)
    ends = ends_ref[...]
    lane = lax.broadcasted_iota(jnp.int32, (srcs, srcs), 1)
    place = jnp.right_shift(ends.astype(jnp.int32), pass_dev.bit_length() - 1)
    low, high = place[:, 0:1], place[:, 1:2]
    second = ends[:, 1:2] > ends[:, 0:1]
    part_ref[...] = jnp.where(lane == low, value[0:srcs], 0.0) + jnp.where(
        (lane == high) & second, value[srcs : 2 * srcs], 0.0
    )
    greeted()

    def rows_of(g):
        return part_ref.at[pl.ds(pl.multiple_of(g * cents, cents), cents)]

    blocks, tops, lines = [], [], []
    for d in range(1, groups):
        peer = lax.rem(me_g + d, groups)
        blocks.append(push(rows_of(peer), part_buf.at[me_g], s1.at[d], r1.at[d], "grp", peer))
    for d in range(1, cents):
        peer = lax.rem(me_c + d, cents)
        tops.append(push(best_ref, best_buf.at[me_c], sb.at[d], rb.at[d], "cent", peer))
        lines.append(push(sum_buf.at[peer], row_buf.at[me_c], s2.at[d], r2.at[d], "cent", peer))
    for copy in blocks:
        copy.start()
    for copy in tops:
        copy.start()
    part_buf[me_g] = part_ref[pl.ds(pl.multiple_of(me_g * cents, cents), cents), :]
    best_buf[me_c] = best_ref[...]
    for copy in blocks:
        copy.wait_recv()
    total = part_buf[0]
    for g in range(1, groups):
        total = total + part_buf[g]
    for c in range(cents):
        sum_buf[c] = total[c : c + 1, :]
    row_buf[me_c] = sum_buf[me_c]
    for copy in lines:
        copy.start()

    for copy in tops:
        copy.wait_recv()
    top = best_buf[0]
    for c in range(1, cents):
        top = jnp.maximum(top, best_buf[c])
    width = token_ref.shape[1]
    for r in range(token_ref.shape[0]):
        token_ref[r : r + 1, :] = top[:, r * width : (r + 1) * width]

    for copy in lines:
        copy.wait_recv()
    line = row_buf[0]
    for c in range(1, cents):
        line = line + row_buf[c]
    half = score_ref.shape[1]
    score_ref[0:1, :] = line[:, 0:half]
    score_ref[1:2, :] = line[:, half : 2 * half]
    for copy in blocks + tops + lines:
        copy.wait_send()


def shards(queries, centroids, candidates, token_codes, resid_words, lengths, levels):
    query_rows, qtok, width = queries.shape
    cent_dev = centroids.shape[0]
    pass_dev, plen = token_codes.shape
    packed = resid_words.shape[1]
    per_device, cand_count = candidates.shape[2:]
    cents, groups = lax.axis_size("cent"), lax.axis_size("grp")
    srcs = cents * groups
    tokens = query_rows * qtok
    block, head = 2048, cent_dev // 2
    tiles = tokens // 256
    mib = 1 << 20
    dma = pltpu.SemaphoreType.DMA
    f32, i32, bf16 = jnp.float32, jnp.int32, jnp.bfloat16
    sds = jax.ShapeDtypeStruct
    hbm = functools.partial(pltpu.with_memory_space_constraint, memory_space=pltpu.HBM)

    table, tail, words, qall, qt, acc, picks, ends, entries = pl.pallas_call(
        functools.partial(search_kernel, cents, groups, pass_dev, block, head, cand_count),
        out_shape=(
            sds((cent_dev, width), f32),
            sds((cent_dev - head, width), bf16),
            sds((pass_dev, packed, width), i32),
            sds((groups, tokens, width), bf16),
            sds((tiles, width, 256), bf16),
            sds((tiles, 8, 256), f32),
            sds((32, plen // 32 * pass_dev), i32),
            sds((srcs, srcs), f32),
            sds((8, srcs), i32),
        ),
        in_specs=[ANY] * 5,
        out_specs=(VMEM,) * 9,
        scratch_shapes=[
            pltpu.VMEM((per_device, cand_count), i32),
            pltpu.VMEM((pass_dev, plen), i32),
            pltpu.VMEM((head, width), bf16),
            pltpu.VMEM((cents, 1, srcs), i32),
            pltpu.VMEM((groups, cents, 1, srcs), i32),
            pltpu.VMEM((srcs, srcs), i32),
            dma((head // block,)),
            dma(((cent_dev - head) // block,)),
            dma,
            dma,
            dma,
            dma,
            dma((cents,)),
            dma((cents,)),
            dma((groups,)),
            dma((groups,)),
            dma((13,)),
            dma((13,)),
        ],
        compiler_params=pltpu.CompilerParams(
            collective_id=0, has_side_effects=True, vmem_limit_bytes=6 * mib
        ),
        name="search",
    )(
        hbm(queries.reshape(tokens, width)),
        hbm(candidates.reshape(per_device, cand_count)),
        hbm(token_codes),
        hbm(centroids),
        hbm(resid_words),
    )

    slots = 2 * srcs
    held = (slots + 1) * (plen // 32) + 2 * UNITS
    embeds, starts, best = pl.pallas_call(
        functools.partial(passage_kernel, cents, groups, pass_dev, plen, OPENING),
        out_shape=(sds((held, 32, width), bf16), sds((slots,), i32), sds((1, tokens), f32)),
        in_specs=[SMEM, SMEM] + [VMEM, ANY] + [VMEM] * 5,
        out_specs=(VMEM, SMEM, VMEM),
        scratch_shapes=[
            pltpu.SMEM((slots * (plen // 32) + UNITS + 4,), i32),
            pltpu.SMEM((pass_dev + 1,), i32),
            pltpu.VMEM((UNITS * 32, width), f32),
            pltpu.VMEM((tiles, 8, 256), f32),
            dma((32,)),
            *[pltpu.SMEM((plen // 32 * pass_dev,), i32) for _ in range(32)],
        ],
        compiler_params=pltpu.CompilerParams(vmem_limit_bytes=2 * mib),
        name="passages",
    )(entries.reshape(8 * srcs), lengths, levels, picks, table, tail, words, qt, acc)

    token_best, scores = pl.pallas_call(
        functools.partial(return_kernel, cents, groups, pass_dev, plen, qtok),
        out_shape=(sds((query_rows, qtok), f32), sds((per_device, cand_count), f32)),
        in_specs=[SMEM] * 3 + [VMEM] * 4,
        out_specs=(VMEM, VMEM),
        scratch_shapes=[
            pltpu.VMEM((srcs, srcs), f32),
            pltpu.VMEM((slots, 128), f32),
            [pltpu.VMEM((128, 128 // qtok * width), bf16) for _ in range(BATCH * qtok // 128)],
            pltpu.VMEM((cents, 1, tokens), f32),
            pltpu.VMEM((groups, cents, srcs), f32),
            pltpu.VMEM((cents, 1, srcs), f32),
            pltpu.VMEM((cents, 1, srcs), f32),
            dma((cents,)),
            dma((cents,)),
            dma((groups,)),
            dma((groups,)),
            dma((cents,)),
            dma((cents,)),
        ],
        compiler_params=pltpu.CompilerParams(
            collective_id=1, has_side_effects=True, vmem_limit_bytes=4 * mib
        ),
        name="returns",
    )(
        entries.reshape(8 * srcs),
        lengths,
        starts,
        ends,
        embeds,
        qall.reshape(groups * query_rows, qtok, width),
        best,
    )
    return token_best, scores.reshape(1, 1, per_device, cand_count)


def solution(mesh):
    placed = (
        P("grp", None, None),
        P("cent", None),
        P("grp", "cent", None, None),
        P(("cent", "grp"), None),
        P(("cent", "grp"), None, None),
        P(("cent", "grp")),
        P(),
    )
    return jax.shard_map(
        shards,
        mesh=mesh,
        in_specs=placed,
        out_specs=(P("grp", None), P("grp", "cent", None, None)),
        check_vma=False,
    )
```

```python
import functools

import jax
import jax.numpy as jnp
from jax import lax
from jax.experimental import pallas as pl
from jax.experimental.pallas import tpu as pltpu
from jax.sharding import PartitionSpec as P

MESH = pl.DeviceIdType.MESH
ANY = pl.BlockSpec(memory_space=pl.ANY)
VMEM = pl.BlockSpec(memory_space=pltpu.VMEM)
SMEM = pl.BlockSpec(memory_space=pltpu.SMEM)
EMPTY = 1 << 20
MASKED = -1000000000.0
UNITS = 8
BATCH = 32
PIECE = 2048
OPENING = 8


def greet(axis_peers):
    barrier = pltpu.get_barrier_semaphore()
    total = 0
    for axis, me, size in axis_peers:
        for d in range(1, size):
            pl.semaphore_signal(
                barrier, inc=1, device_id={axis: lax.rem(me + d, size)}, device_id_type=MESH
            )
            total += 1
    return lambda: pl.semaphore_wait(barrier, total)


def push(src, dst, send, recv, axis, peer):
    return pltpu.make_async_remote_copy(
        src_ref=src,
        dst_ref=dst,
        send_sem=send,
        recv_sem=recv,
        device_id={axis: peer},
        device_id_type=MESH,
    )


def search_kernel(
    cents, groups, pass_dev, block, head, cand_count,
    q_hbm, cand_hbm, codes_hbm, cent_hbm, words_hbm,
    table_ref, tail_ref, words_ref, qall_ref, qt_ref, acc_ref, picks_ref, ends_ref, entry_ref,
    cand_ref, codes_ref, head_buf, row_buf, all_buf, rows, csem, tsem, wsem, own_sem, cand_sem, codes_sem, s1, r1, s2, r2, sq, rq,
):
    me_c, me_g = lax.axis_index("cent"), lax.axis_index("grp")
    partner = me_g + 1 - 2 * lax.rem(me_g, 2)
    ahead, behind = lax.rem(me_g + 2, groups), lax.rem(me_g + groups - 2, groups)
    across = lax.rem(me_g + 4, groups)
    steps = head // block
    later = tail_ref.shape[0] // block
    tiles, width = qt_ref.shape[0], qt_ref.shape[2]
    half = q_hbm.shape[0] // 2
    mine_q = qall_ref.at[me_g]

    cand_copy = pltpu.make_async_copy(cand_hbm, cand_ref, cand_sem)
    cand_copy.start()
    own = pltpu.make_async_copy(q_hbm, mine_q, own_sem)
    own.start()
    fetch = [
        pltpu.make_async_copy(
            cent_hbm.at[pl.ds(b * block, block)], head_buf.at[pl.ds(b * block, block)], csem.at[b]
        )
        for b in range(steps)
    ]
    fetch_tail = [
        pltpu.make_async_copy(
            cent_hbm.at[pl.ds(head + b * block, block)], tail_ref.at[pl.ds(b * block, block)], tsem.at[b]
        )
        for b in range(later)
    ]
    codes_copy = pltpu.make_async_copy(codes_hbm, codes_ref, codes_sem)
    words_copy = pltpu.make_async_copy(words_hbm, words_ref, wsem)
    cand_copy.wait()
    row_buf[me_c] = jnp.concatenate([cand_ref[0:1, :], cand_ref[1:2, :]], axis=1)
    greeted = greet((("cent", me_c, cents), ("grp", me_g, groups)))
    own.wait()
    fetch[0].start()
    codes_copy.start()
    for copy in fetch[1:] + fetch_tail:
        copy.start()
    words_copy.start()
    for t in range(tiles):
        qt_ref[t] = qall_ref[me_g, t * width : (t + 1) * width, :].T
    acc_ref[...] = jnp.full(acc_ref.shape, -jnp.inf, jnp.float32)
    codes_copy.wait()
    by_token = codes_ref[...].T
    for part in range(codes_ref.shape[1] // 32):
        span = slice(part * pass_dev, (part + 1) * pass_dev)
        picks_ref[:, span] = by_token[part * 32 : (part + 1) * 32, :]
    greeted()

    gather_rows = [
        push(row_buf.at[me_c], row_buf.at[me_c], s1.at[d], r1.at[d], "cent", lax.rem(me_c + d, cents))
        for d in range(1, cents)
    ]
    gather_groups = [
        push(row_buf, all_buf.at[me_g], s2.at[d], r2.at[d], "grp", lax.rem(me_g + d, groups))
        for d in range(1, groups)
    ]

    low, high = pl.ds(0, half), pl.ds(half, half)
    lanes = iter(range(sq.shape[0]))

    def hand(block_of, span, peer):
        k = next(lanes)
        held = qall_ref.at[block_of, span]
        return push(held, held, sq.at[k], rq.at[k], "grp", peer)

    ahead_low, behind_high = hand(me_g, low, ahead), hand(me_g, high, behind)
    ahead_high, behind_low = hand(me_g, high, ahead), hand(me_g, low, behind)
    to_partner = hand(me_g, pl.ds(0, 2 * half), partner)
    relay_ahead, relay_behind = hand(behind, low, ahead), hand(ahead, high, behind)
    shares = [
        hand(block_of, span, partner)
        for block_of, span in (
            (behind, low), (ahead, high), (behind, high), (ahead, low), (across, low), (across, high)
        )
    ]

    for copy in gather_rows:
        copy.start()
    for copy in (ahead_low, behind_high, ahead_high, behind_low, to_partner):
        copy.start()

    def step(b, _):
        here = pl.ds(pl.multiple_of(b * block, block), block)
        pltpu.make_async_copy(cent_hbm.at[here], head_buf.at[here], csem.at[b]).wait()

        @pl.when(b == 4)
        def _():
            for copy in gather_rows:
                copy.wait_recv()
            for copy in gather_groups:
                copy.start()

        @pl.when(b == 3)
        def _():
            ahead_low.wait_recv()
            relay_ahead.start()
            shares[0].start()
            behind_high.wait_recv()
            relay_behind.start()
            shares[1].start()

        @pl.when(b == 5)
        def _():
            ahead_high.wait_recv()
            shares[2].start()
            behind_low.wait_recv()
            shares[3].start()

        @pl.when(b == 7)
        def _():
            relay_ahead.wait_recv()
            shares[4].start()
            relay_behind.wait_recv()
            shares[5].start()

        beyond = pl.ds(pl.multiple_of(head + b * block, block), block)
        pltpu.make_async_copy(cent_hbm.at[beyond], tail_ref.at[here], tsem.at[b]).wait()
        table_ref[beyond, :] = tail_ref[here, :].astype(jnp.float32)
        table_ref[here, :] = head_buf[here, :].astype(jnp.float32)
        for t in range(tiles):
            scores = jnp.dot(head_buf[here, :], qt_ref[t], preferred_element_type=jnp.float32)
            top = jnp.max(scores.reshape(block // 8, 8, width), axis=0)
            acc_ref[t] = jnp.maximum(acc_ref[t], top)
        return 0

    lax.fori_loop(0, steps, step, 0)
    for copy in gather_groups:
        copy.wait_recv()
    all_buf[me_g] = row_buf[...]
    for g in range(groups):
        for c in range(cents):
            rows[pl.ds(g * cents + c, 1), :] = all_buf[g, c]
    found = rows[...]
    lane = lax.broadcasted_iota(jnp.int32, found.shape, 1)
    mine = jnp.right_shift(found, pass_dev.bit_length() - 1) == me_c * groups + me_g
    packed = (lane * pass_dev + jnp.bitwise_and(found, pass_dev - 1)).astype(jnp.float32)
    first = jnp.min(jnp.where(mine, packed, float(EMPTY)), axis=1, keepdims=True)
    last = jnp.max(jnp.where(mine, packed, -1.0), axis=1, keepdims=True)
    ends = jnp.where(lane == 0, first, jnp.where(lane == 1, last, 0.0))
    ends_ref[...] = ends
    turned = ends.T[0:8, :].astype(jnp.int32)
    source = lax.broadcasted_iota(jnp.int32, turned.shape, 1)
    slot = lax.broadcasted_iota(jnp.int32, turned.shape, 0)
    other = jnp.where(slot == 1, jnp.broadcast_to(turned[0:1, :], turned.shape), -1)
    there = (turned < EMPTY) & (turned > other)
    query = 2 * source + jnp.right_shift(turned, (pass_dev * cand_count).bit_length() - 1)
    entry = jnp.bitwise_and(turned, pass_dev - 1) + pass_dev * (
        query + 2 * cents * groups * (slot * cents * groups + source)
    )
    entry_ref[...] = jnp.where(there, entry, -1)

    words_copy.wait()
    for copy in gather_rows + gather_groups:
        copy.wait_send()
    for copy in (ahead_low, behind_high, ahead_high, behind_low, relay_ahead, relay_behind):
        copy.wait_send()
    for copy in [to_partner] + shares:
        copy.wait()


def passage_kernel(
    cents, groups, pass_dev, plen, opening,
    entries, len_ref, lev_ref, picks_ref, table, tail, words, qt_ref, acc_in,
    embeds, starts, best_ref,
    units, seen, dense, acc, csem, *picks,
):
    srcs = groups * cents
    tiles = qt_ref.shape[0]
    rows_of_piece = PIECE
    pieces = tail.shape[0] // rows_of_piece * tiles
    loads = [
        pltpu.make_async_copy(picks_ref.at[r], picks[r], csem.at[r]) for r in range(len(picks))
    ]
    for copy in loads:
        copy.start()
    acc[...] = acc_in[...]

    def piece(m):
        t = lax.rem(m, tiles)
        start = pl.multiple_of(m // tiles * rows_of_piece, rows_of_piece)
        scores = jnp.dot(
            tail[pl.ds(start, rows_of_piece), :], qt_ref[t], preferred_element_type=jnp.float32
        )
        top = jnp.max(scores.reshape(rows_of_piece // 8, 8, scores.shape[1]), axis=0)
        acc[t] = jnp.maximum(acc[t], top)

    def collect(src, used):
        pair = [entries[slot * srcs + src] for slot in range(2)]
        there = [entry >= 0 for entry in pair]
        owned = [jnp.bitwise_and(entry, pass_dev - 1) for entry in pair]
        marks = [jnp.where(ok, passage, pass_dev) for ok, passage in zip(there, owned)]
        known = [seen[mark] for mark in marks]
        sizes = [jnp.right_shift(len_ref[passage] + 31, 5) for passage in owned]
        for n in range(2):
            at = jnp.where(known[n] < 0, used, known[n])
            starts[n * srcs + src] = jnp.where(there[n], at, 0) + UNITS
            seen[marks[n]] = at
            for part in range(plen // 32):
                units[used + part] = owned[n] + part * pass_dev
            used = used + jnp.where(there[n] & (known[n] < 0), sizes[n], 0)
        return used

    def open_step(m, state):
        piece(m)
        for k in range(srcs // opening):
            state = collect(m * (srcs // opening) + k, state)
        return state

    def forget(k, _):
        seen[k] = -1
        return 0

    seen[pass_dev] = 0
    lax.fori_loop(0, pass_dev, forget, 0, unroll=16)
    used = lax.fori_loop(0, opening, open_step, jnp.int32(0))
    for pad in range(UNITS):
        units[used + pad] = 0
    for copy in loads:
        copy.wait()

    sub = lax.broadcasted_iota(jnp.int32, (8, 128), 0)
    level = [jnp.broadcast_to(lev_ref[k : k + 1, :], (8, 128)) for k in range(4)]

    def embed(at):
        passage = jnp.bitwise_and(at, pass_dev - 1)
        part = jnp.right_shift(at, pass_dev.bit_length() - 1)
        word = words[passage, pl.ds(pl.multiple_of(part * 8, 8), 8), :]
        tiles = []
        for j in range(4):
            rows = None
            for s in range(8):
                row = table[pl.ds(picks[4 * s + j][at], 1), :]
                row = jnp.broadcast_to(row, (8, 128))
                rows = row if rows is None else jnp.where(sub == s, row, rows)
            low = jnp.bitwise_and(word, 1 << (2 * j)) != 0
            high = jnp.bitwise_and(word, 2 << (2 * j)) != 0
            residual = jnp.where(
                high, jnp.where(low, level[3], level[2]), jnp.where(low, level[1], level[0])
            )
            tiles.append(rows + residual)
        return tiles

    def finish(turn):
        for k in range(UNITS):
            tiles = []
            for j in range(4):
                value = dense[k * 32 + j * 8 : k * 32 + j * 8 + 8, :]
                squares = jnp.sum(value * value, axis=1, keepdims=True)
                tiles.append(value * lax.rsqrt(squares + 1e-06))
            embeds[turn * UNITS + k] = jnp.concatenate(tiles, axis=0).astype(jnp.bfloat16)

    def embed_step(i, _):
        finish(i)
        for k in range(UNITS):
            for j, tile in enumerate(embed(units[i * UNITS + k])):
                dense[k * 32 + j * 8 : k * 32 + j * 8 + 8, :] = tile
        return 0

    def piece_step(m, _):
        piece(m)
        return 0

    def both_step(i, _):
        piece(opening + i)
        return embed_step(i, 0)

    turns = pl.cdiv(used, UNITS)
    shared = jnp.minimum(turns, pieces - opening)
    lax.fori_loop(0, shared, both_step, 0)
    lax.fori_loop(shared, turns, embed_step, 0)
    lax.fori_loop(opening + shared, pieces, piece_step, 0)
    finish(turns)
    for k in range(plen // 32):
        embeds[(turns + 1) * UNITS + k] = jnp.zeros(embeds.shape[1:], embeds.dtype)
    for t in range(tiles):
        width = acc.shape[2]
        best_ref[:, t * width : (t + 1) * width] = jnp.max(acc[t], axis=0, keepdims=True)


def return_kernel(
    cents, groups, pass_dev, plen, qtok,
    entries, len_ref, starts, ends_ref, embeds, q_ref, best_ref,
    token_ref, score_ref,
    part_ref, totals, spread, best_buf, part_buf, sum_buf, row_buf, sb, rb, s1, r1, s2, r2,
):
    me_c, me_g = lax.axis_index("cent"), lax.axis_index("grp")
    srcs = cents * groups
    greeted = greet((("cent", me_c, cents), ("grp", me_g, groups)))
    lane_q = lax.broadcasted_iota(jnp.int32, (8, 128), 1)
    four = 128 // qtok

    sub = lax.broadcasted_iota(jnp.int32, (8, 128), 0)
    for wide in spread:
        wide[...] = jnp.zeros(wide.shape, wide.dtype)

    def score_step(batch, _):
        for k, wide in enumerate(spread):
            limit, held = None, []
            for n in range(four):
                i = batch * BATCH + k * four + n
                entry = entries[i]
                query = jnp.bitwise_and(jnp.right_shift(entry, pass_dev.bit_length() - 1), 2 * srcs - 1)
                length = len_ref[jnp.bitwise_and(entry, pass_dev - 1)]
                wide[n * qtok : (n + 1) * qtok, n * 128 : (n + 1) * 128] = q_ref[query]
                limit = length if limit is None else jnp.where(lane_q >= n * qtok, length, limit)
                first = starts[i]
                held.append(
                    jnp.concatenate([embeds[first + part] for part in range(plen // 32)], axis=0)
                )
            scores = lax.dot_general(
                jnp.concatenate(held, axis=1), wide[...], (((1,), (1,)), ((), ())), preferred_element_type=jnp.float32
            )
            top = None
            for part in range(plen // 32):
                for j in range(4):
                    at = part * 32 + j * 8
                    inside = 4 * sub + (part * 32 + j) < limit
                    tile = jnp.where(inside, scores[at : at + 8], MASKED)
                    top = tile if top is None else jnp.maximum(top, tile)
            line = jnp.max(top, axis=0, keepdims=True)
            for n in range(four):
                own = (lane_q[0:1] >= n * qtok) & (lane_q[0:1] < (n + 1) * qtok)
                totals[pl.ds(batch * BATCH + k * four + n, 1), :] = jnp.where(own, line, 0.0)
        return 0

    lax.fori_loop(0, 2 * srcs // BATCH, score_step, 0)

    value = jnp.sum(totals[...], axis=1, keepdims=True) * (1.0 / qtok)
    ends = ends_ref[...]
    lane = lax.broadcasted_iota(jnp.int32, (srcs, srcs), 1)
    place = jnp.right_shift(ends.astype(jnp.int32), pass_dev.bit_length() - 1)
    low, high = place[:, 0:1], place[:, 1:2]
    second = ends[:, 1:2] > ends[:, 0:1]
    part_ref[...] = jnp.where(lane == low, value[0:srcs], 0.0) + jnp.where(
        (lane == high) & second, value[srcs : 2 * srcs], 0.0
    )
    greeted()

    def rows_of(g):
        return part_ref.at[pl.ds(pl.multiple_of(g * cents, cents), cents)]

    blocks, tops, lines = [], [], []
    for d in range(1, groups):
        peer = lax.rem(me_g + d, groups)
        blocks.append(push(rows_of(peer), part_buf.at[me_g], s1.at[d], r1.at[d], "grp", peer))
    for d in range(1, cents):
        peer = lax.rem(me_c + d, cents)
        tops.append(push(best_ref, best_buf.at[me_c], sb.at[d], rb.at[d], "cent", peer))
        lines.append(push(sum_buf.at[peer], row_buf.at[me_c], s2.at[d], r2.at[d], "cent", peer))
    for copy in blocks:
        copy.start()
    for copy in tops:
        copy.start()
    part_buf[me_g] = part_ref[pl.ds(pl.multiple_of(me_g * cents, cents), cents), :]
    best_buf[me_c] = best_ref[...]
    for copy in blocks:
        copy.wait_recv()
    total = part_buf[0]
    for g in range(1, groups):
        total = total + part_buf[g]
    for c in range(cents):
        sum_buf[c] = total[c : c + 1, :]
    row_buf[me_c] = sum_buf[me_c]
    for copy in lines:
        copy.start()

    for copy in tops:
        copy.wait_recv()
    top = best_buf[0]
    for c in range(1, cents):
        top = jnp.maximum(top, best_buf[c])
    width = token_ref.shape[1]
    for r in range(token_ref.shape[0]):
        token_ref[r : r + 1, :] = top[:, r * width : (r + 1) * width]

    for copy in lines:
        copy.wait_recv()
    line = row_buf[0]
    for c in range(1, cents):
        line = line + row_buf[c]
    half = score_ref.shape[1]
    score_ref[0:1, :] = line[:, 0:half]
    score_ref[1:2, :] = line[:, half : 2 * half]
    for copy in blocks + tops + lines:
        copy.wait_send()


def shards(queries, centroids, candidates, token_codes, resid_words, lengths, levels):
    query_rows, qtok, width = queries.shape
    cent_dev = centroids.shape[0]
    pass_dev, plen = token_codes.shape
    packed = resid_words.shape[1]
    per_device, cand_count = candidates.shape[2:]
    cents, groups = lax.axis_size("cent"), lax.axis_size("grp")
    srcs = cents * groups
    tokens = query_rows * qtok
    block, head = 2048, cent_dev // 2
    tiles = tokens // 256
    mib = 1 << 20
    dma = pltpu.SemaphoreType.DMA
    f32, i32, bf16 = jnp.float32, jnp.int32, jnp.bfloat16
    sds = jax.ShapeDtypeStruct
    hbm = functools.partial(pltpu.with_memory_space_constraint, memory_space=pltpu.HBM)

    table, tail, words, qall, qt, acc, picks, ends, entries = pl.pallas_call(
        functools.partial(search_kernel, cents, groups, pass_dev, block, head, cand_count),
        out_shape=(
            sds((cent_dev, width), f32),
            sds((cent_dev - head, width), bf16),
            sds((pass_dev, packed, width), i32),
            sds((groups, tokens, width), bf16),
            sds((tiles, width, 256), bf16),
            sds((tiles, 8, 256), f32),
            sds((32, plen // 32 * pass_dev), i32),
            sds((srcs, srcs), f32),
            sds((8, srcs), i32),
        ),
        in_specs=[ANY] * 5,
        out_specs=(VMEM,) * 9,
        scratch_shapes=[
            pltpu.VMEM((per_device, cand_count), i32),
            pltpu.VMEM((pass_dev, plen), i32),
            pltpu.VMEM((head, width), bf16),
            pltpu.VMEM((cents, 1, srcs), i32),
            pltpu.VMEM((groups, cents, 1, srcs), i32),
            pltpu.VMEM((srcs, srcs), i32),
            dma((head // block,)),
            dma(((cent_dev - head) // block,)),
            dma,
            dma,
            dma,
            dma,
            dma((cents,)),
            dma((cents,)),
            dma((groups,)),
            dma((groups,)),
            dma((13,)),
            dma((13,)),
        ],
        compiler_params=pltpu.CompilerParams(
            collective_id=0, has_side_effects=True, vmem_limit_bytes=6 * mib
        ),
        name="search",
    )(
        hbm(queries.reshape(tokens, width)),
        hbm(candidates.reshape(per_device, cand_count)),
        hbm(token_codes),
        hbm(centroids),
        hbm(resid_words),
    )

    slots = 2 * srcs
    held = (slots + 1) * (plen // 32) + 2 * UNITS
    embeds, starts, best = pl.pallas_call(
        functools.partial(passage_kernel, cents, groups, pass_dev, plen, OPENING),
        out_shape=(sds((held, 32, width), bf16), sds((slots,), i32), sds((1, tokens), f32)),
        in_specs=[SMEM, SMEM] + [VMEM, ANY] + [VMEM] * 5,
        out_specs=(VMEM, SMEM, VMEM),
        scratch_shapes=[
            pltpu.SMEM((slots * (plen // 32) + UNITS + 4,), i32),
            pltpu.SMEM((pass_dev + 1,), i32),
            pltpu.VMEM((UNITS * 32, width), f32),
            pltpu.VMEM((tiles, 8, 256), f32),
            dma((32,)),
            *[pltpu.SMEM((plen // 32 * pass_dev,), i32) for _ in range(32)],
        ],
        compiler_params=pltpu.CompilerParams(vmem_limit_bytes=2 * mib),
        name="passages",
    )(entries.reshape(8 * srcs), lengths, levels, picks, table, tail, words, qt, acc)

    token_best, scores = pl.pallas_call(
        functools.partial(return_kernel, cents, groups, pass_dev, plen, qtok),
        out_shape=(sds((query_rows, qtok), f32), sds((per_device, cand_count), f32)),
        in_specs=[SMEM] * 3 + [VMEM] * 4,
        out_specs=(VMEM, VMEM),
        scratch_shapes=[
            pltpu.VMEM((srcs, srcs), f32),
            pltpu.VMEM((slots, 128), f32),
            [pltpu.VMEM((128, 128 // qtok * width), bf16) for _ in range(BATCH * qtok // 128)],
            pltpu.VMEM((cents, 1, tokens), f32),
            pltpu.VMEM((groups, cents, srcs), f32),
            pltpu.VMEM((cents, 1, srcs), f32),
            pltpu.VMEM((cents, 1, srcs), f32),
            dma((cents,)),
            dma((cents,)),
            dma((groups,)),
            dma((groups,)),
            dma((cents,)),
            dma((cents,)),
        ],
        compiler_params=pltpu.CompilerParams(
            collective_id=1, has_side_effects=True, vmem_limit_bytes=4 * mib
        ),
        name="returns",
    )(
        entries.reshape(8 * srcs),
        lengths,
        starts,
        ends,
        embeds,
        qall.reshape(groups * query_rows, qtok, width),
        best,
    )
    return token_best, scores.reshape(1, 1, per_device, cand_count)


def solution(mesh):
    placed = (
        P("grp", None, None),
        P("cent", None),
        P("grp", "cent", None, None),
        P(("cent", "grp"), None),
        P(("cent", "grp"), None, None),
        P(("cent", "grp")),
        P(),
    )
    return jax.shard_map(
        shards,
        mesh=mesh,
        in_specs=placed,
        out_specs=(P("grp", None), P("grp", "cent", None, None)),
        check_vma=False,
    )
```

```python
import functools

import jax
import jax.numpy as jnp
from jax import lax
from jax.experimental import pallas as pl
from jax.experimental.pallas import tpu as pltpu
from jax.sharding import PartitionSpec as P

MESH = pl.DeviceIdType.MESH
ANY = pl.BlockSpec(memory_space=pl.ANY)
VMEM = pl.BlockSpec(memory_space=pltpu.VMEM)
SMEM = pl.BlockSpec(memory_space=pltpu.SMEM)
EMPTY = 1 << 20
MASKED = -1000000000.0
UNITS = 16
BATCH = 64
PIECE = 2048
OPENING = 8


def greet(axis_peers):
    barrier = pltpu.get_barrier_semaphore()
    total = 0
    for axis, me, size in axis_peers:
        for d in range(1, size):
            pl.semaphore_signal(
                barrier, inc=1, device_id={axis: lax.rem(me + d, size)}, device_id_type=MESH
            )
            total += 1
    return lambda: pl.semaphore_wait(barrier, total)


def push(src, dst, send, recv, axis, peer):
    return pltpu.make_async_remote_copy(
        src_ref=src,
        dst_ref=dst,
        send_sem=send,
        recv_sem=recv,
        device_id={axis: peer},
        device_id_type=MESH,
    )


def search_kernel(
    cents, groups, pass_dev, block, head, cand_count,
    q_hbm, cand_hbm, codes_hbm, cent_hbm, words_hbm,
    table_ref, tail_ref, words_ref, qall_ref, qt_ref, acc_ref, picks_ref, ends_ref, entry_ref,
    cand_ref, codes_ref, head_buf, row_buf, all_buf, rows, csem, tsem, wsem, own_sem, cand_sem, codes_sem, s1, r1, s2, r2, sq, rq,
):
    me_c, me_g = lax.axis_index("cent"), lax.axis_index("grp")
    partner = me_g + 1 - 2 * lax.rem(me_g, 2)
    ahead, behind = lax.rem(me_g + 2, groups), lax.rem(me_g + groups - 2, groups)
    across = lax.rem(me_g + 4, groups)
    steps = head // block
    later = tail_ref.shape[0] // block
    tiles, width = qt_ref.shape[0], qt_ref.shape[2]
    half = q_hbm.shape[0] // 2
    mine_q = qall_ref.at[me_g]

    cand_copy = pltpu.make_async_copy(cand_hbm, cand_ref, cand_sem)
    cand_copy.start()
    own = pltpu.make_async_copy(q_hbm, mine_q, own_sem)
    own.start()
    fetch = [
        pltpu.make_async_copy(
            cent_hbm.at[pl.ds(b * block, block)], head_buf.at[pl.ds(b * block, block)], csem.at[b]
        )
        for b in range(steps)
    ]
    fetch_tail = [
        pltpu.make_async_copy(
            cent_hbm.at[pl.ds(head + b * block, block)], tail_ref.at[pl.ds(b * block, block)], tsem.at[b]
        )
        for b in range(later)
    ]
    codes_copy = pltpu.make_async_copy(codes_hbm, codes_ref, codes_sem)
    words_copy = pltpu.make_async_copy(words_hbm, words_ref, wsem)
    cand_copy.wait()
    row_buf[me_c] = jnp.concatenate([cand_ref[0:1, :], cand_ref[1:2, :]], axis=1)
    greeted = greet((("cent", me_c, cents), ("grp", me_g, groups)))
    own.wait()
    fetch[0].start()
    codes_copy.start()
    for copy in fetch[1:] + fetch_tail:
        copy.start()
    words_copy.start()
    for t in range(tiles):
        qt_ref[t] = qall_ref[me_g, t * width : (t + 1) * width, :].T
    acc_ref[...] = jnp.full(acc_ref.shape, -jnp.inf, jnp.float32)
    codes_copy.wait()
    by_token = codes_ref[...].T
    for part in range(codes_ref.shape[1] // 32):
        span = slice(part * pass_dev, (part + 1) * pass_dev)
        picks_ref[:, span] = by_token[part * 32 : (part + 1) * 32, :]
    greeted()

    gather_rows = [
        push(row_buf.at[me_c], row_buf.at[me_c], s1.at[d], r1.at[d], "cent", lax.rem(me_c + d, cents))
        for d in range(1, cents)
    ]
    gather_groups = [
        push(row_buf, all_buf.at[me_g], s2.at[d], r2.at[d], "grp", lax.rem(me_g + d, groups))
        for d in range(1, groups)
    ]

    low, high = pl.ds(0, half), pl.ds(half, half)
    lanes = iter(range(sq.shape[0]))

    def hand(block_of, span, peer):
        k = next(lanes)
        held = qall_ref.at[block_of, span]
        return push(held, held, sq.at[k], rq.at[k], "grp", peer)

    ahead_low, behind_high = hand(me_g, low, ahead), hand(me_g, high, behind)
    ahead_high, behind_low = hand(me_g, high, ahead), hand(me_g, low, behind)
    to_partner = hand(me_g, pl.ds(0, 2 * half), partner)
    relay_ahead, relay_behind = hand(behind, low, ahead), hand(ahead, high, behind)
    shares = [
        hand(block_of, span, partner)
        for block_of, span in (
            (behind, low), (ahead, high), (behind, high), (ahead, low), (across, low), (across, high)
        )
    ]

    for copy in gather_rows:
        copy.start()
    for copy in (ahead_low, behind_high, ahead_high, behind_low, to_partner):
        copy.start()

    def step(b, _):
        here = pl.ds(pl.multiple_of(b * block, block), block)
        pltpu.make_async_copy(cent_hbm.at[here], head_buf.at[here], csem.at[b]).wait()

        @pl.when(b == 4)
        def _():
            for copy in gather_rows:
                copy.wait_recv()
            for copy in gather_groups:
                copy.start()

        @pl.when(b == 3)
        def _():
            ahead_low.wait_recv()
            relay_ahead.start()
            shares[0].start()
            behind_high.wait_recv()
            relay_behind.start()
            shares[1].start()

        @pl.when(b == 5)
        def _():
            ahead_high.wait_recv()
            shares[2].start()
            behind_low.wait_recv()
            shares[3].start()

        @pl.when(b == 7)
        def _():
            relay_ahead.wait_recv()
            shares[4].start()
            relay_behind.wait_recv()
            shares[5].start()

        beyond = pl.ds(pl.multiple_of(head + b * block, block), block)
        pltpu.make_async_copy(cent_hbm.at[beyond], tail_ref.at[here], tsem.at[b]).wait()
        table_ref[beyond, :] = tail_ref[here, :].astype(jnp.float32)
        table_ref[here, :] = head_buf[here, :].astype(jnp.float32)
        for t in range(tiles):
            scores = jnp.dot(head_buf[here, :], qt_ref[t], preferred_element_type=jnp.float32)
            top = jnp.max(scores.reshape(block // 8, 8, width), axis=0)
            acc_ref[t] = jnp.maximum(acc_ref[t], top)
        return 0

    lax.fori_loop(0, steps, step, 0)
    for copy in gather_groups:
        copy.wait_recv()
    all_buf[me_g] = row_buf[...]
    for g in range(groups):
        for c in range(cents):
            rows[pl.ds(g * cents + c, 1), :] = all_buf[g, c]
    found = rows[...]
    lane = lax.broadcasted_iota(jnp.int32, found.shape, 1)
    mine = jnp.right_shift(found, pass_dev.bit_length() - 1) == me_c * groups + me_g
    packed = (lane * pass_dev + jnp.bitwise_and(found, pass_dev - 1)).astype(jnp.float32)
    first = jnp.min(jnp.where(mine, packed, float(EMPTY)), axis=1, keepdims=True)
    last = jnp.max(jnp.where(mine, packed, -1.0), axis=1, keepdims=True)
    ends = jnp.where(lane == 0, first, jnp.where(lane == 1, last, 0.0))
    ends_ref[...] = ends
    turned = ends.T[0:8, :].astype(jnp.int32)
    source = lax.broadcasted_iota(jnp.int32, turned.shape, 1)
    slot = lax.broadcasted_iota(jnp.int32, turned.shape, 0)
    other = jnp.where(slot == 1, jnp.broadcast_to(turned[0:1, :], turned.shape), -1)
    there = (turned < EMPTY) & (turned > other)
    query = 2 * source + jnp.right_shift(turned, (pass_dev * cand_count).bit_length() - 1)
    entry = jnp.bitwise_and(turned, pass_dev - 1) + pass_dev * (
        query + 2 * cents * groups * (slot * cents * groups + source)
    )
    entry_ref[...] = jnp.where(there, entry, -1)

    words_copy.wait()
    for copy in gather_rows + gather_groups:
        copy.wait_send()
    for copy in (ahead_low, behind_high, ahead_high, behind_low, relay_ahead, relay_behind):
        copy.wait_send()
    for copy in [to_partner] + shares:
        copy.wait()


def passage_kernel(
    cents, groups, pass_dev, plen, opening,
    entries, len_ref, lev_ref, picks_ref, table, tail, words, qt_ref, acc_in,
    embeds, starts, best_ref,
    units, seen, dense, acc, csem, *picks,
):
    srcs = groups * cents
    tiles = qt_ref.shape[0]
    rows_of_piece = PIECE
    pieces = tail.shape[0] // rows_of_piece * tiles
    loads = [
        pltpu.make_async_copy(picks_ref.at[r], picks[r], csem.at[r]) for r in range(len(picks))
    ]
    for copy in loads:
        copy.start()
    acc[...] = acc_in[...]

    def piece(m):
        t = lax.rem(m, tiles)
        start = pl.multiple_of(m // tiles * rows_of_piece, rows_of_piece)
        scores = jnp.dot(
            tail[pl.ds(start, rows_of_piece), :], qt_ref[t], preferred_element_type=jnp.float32
        )
        top = jnp.max(scores.reshape(rows_of_piece // 8, 8, scores.shape[1]), axis=0)
        acc[t] = jnp.maximum(acc[t], top)

    def collect(src, used):
        pair = [entries[slot * srcs + src] for slot in range(2)]
        there = [entry >= 0 for entry in pair]
        owned = [jnp.bitwise_and(entry, pass_dev - 1) for entry in pair]
        marks = [jnp.where(ok, passage, pass_dev) for ok, passage in zip(there, owned)]
        known = [seen[mark] for mark in marks]
        sizes = [jnp.right_shift(len_ref[passage] + 31, 5) for passage in owned]
        for n in range(2):
            at = jnp.where(known[n] < 0, used, known[n])
            starts[n * srcs + src] = jnp.where(there[n], at, 0) + UNITS
            seen[marks[n]] = at
            for part in range(plen // 32):
                units[used + part] = owned[n] + part * pass_dev
            used = used + jnp.where(there[n] & (known[n] < 0), sizes[n], 0)
        return used

    def open_step(m, state):
        piece(m)
        for k in range(srcs // opening):
            state = collect(m * (srcs // opening) + k, state)
        return state

    def forget(k, _):
        seen[k] = -1
        return 0

    seen[pass_dev] = 0
    lax.fori_loop(0, pass_dev, forget, 0, unroll=16)
    used = lax.fori_loop(0, opening, open_step, jnp.int32(0))
    for pad in range(UNITS):
        units[used + pad] = 0
    for copy in loads:
        copy.wait()

    sub = lax.broadcasted_iota(jnp.int32, (8, 128), 0)
    level = [jnp.broadcast_to(lev_ref[k : k + 1, :], (8, 128)) for k in range(4)]

    def embed(at):
        passage = jnp.bitwise_and(at, pass_dev - 1)
        part = jnp.right_shift(at, pass_dev.bit_length() - 1)
        word = words[passage, pl.ds(pl.multiple_of(part * 8, 8), 8), :]
        tiles = []
        for j in range(4):
            rows = None
            for s in range(8):
                row = table[pl.ds(picks[4 * s + j][at], 1), :]
                row = jnp.broadcast_to(row, (8, 128))
                rows = row if rows is None else jnp.where(sub == s, row, rows)
            low = jnp.bitwise_and(word, 1 << (2 * j)) != 0
            high = jnp.bitwise_and(word, 2 << (2 * j)) != 0
            residual = jnp.where(
                high, jnp.where(low, level[3], level[2]), jnp.where(low, level[1], level[0])
            )
            tiles.append(rows + residual)
        return tiles

    def finish(turn):
        for k in range(UNITS):
            tiles = []
            for j in range(4):
                value = dense[k * 32 + j * 8 : k * 32 + j * 8 + 8, :]
                squares = jnp.sum(value * value, axis=1, keepdims=True)
                tiles.append(value * lax.rsqrt(squares + 1e-06))
            embeds[turn * UNITS + k] = jnp.concatenate(tiles, axis=0).astype(jnp.bfloat16)

    def embed_step(i, _):
        finish(i)
        for k in range(UNITS):
            for j, tile in enumerate(embed(units[i * UNITS + k])):
                dense[k * 32 + j * 8 : k * 32 + j * 8 + 8, :] = tile
        return 0

    def piece_step(m, _):
        piece(m)
        return 0

    def both_step(i, _):
        piece(opening + i)
        return embed_step(i, 0)

    turns = pl.cdiv(used, UNITS)
    shared = jnp.minimum(turns, pieces - opening)
    lax.fori_loop(0, shared, both_step, 0)
    lax.fori_loop(shared, turns, embed_step, 0)
    lax.fori_loop(opening + shared, pieces, piece_step, 0)
    finish(turns)
    for k in range(plen // 32):
        embeds[(turns + 1) * UNITS + k] = jnp.zeros(embeds.shape[1:], embeds.dtype)
    for t in range(tiles):
        width = acc.shape[2]
        best_ref[:, t * width : (t + 1) * width] = jnp.max(acc[t], axis=0, keepdims=True)


def return_kernel(
    cents, groups, pass_dev, plen, qtok,
    entries, len_ref, starts, ends_ref, embeds, q_ref, best_ref,
    token_ref, score_ref,
    part_ref, totals, spread, best_buf, part_buf, sum_buf, row_buf, sb, rb, s1, r1, s2, r2,
):
    me_c, me_g = lax.axis_index("cent"), lax.axis_index("grp")
    srcs = cents * groups
    greeted = greet((("cent", me_c, cents), ("grp", me_g, groups)))
    lane_q = lax.broadcasted_iota(jnp.int32, (8, 128), 1)
    four = 128 // qtok

    sub = lax.broadcasted_iota(jnp.int32, (8, 128), 0)
    for wide in spread:
        wide[...] = jnp.zeros(wide.shape, wide.dtype)

    def score_step(batch, _):
        for k, wide in enumerate(spread):
            limit, held = None, []
            for n in range(four):
                i = batch * BATCH + k * four + n
                entry = entries[i]
                query = jnp.bitwise_and(jnp.right_shift(entry, pass_dev.bit_length() - 1), 2 * srcs - 1)
                length = len_ref[jnp.bitwise_and(entry, pass_dev - 1)]
                wide[n * qtok : (n + 1) * qtok, n * 128 : (n + 1) * 128] = q_ref[query]
                limit = length if limit is None else jnp.where(lane_q >= n * qtok, length, limit)
                first = starts[i]
                held.append(
                    jnp.concatenate([embeds[first + part] for part in range(plen // 32)], axis=0)
                )
            scores = lax.dot_general(
                jnp.concatenate(held, axis=1), wide[...], (((1,), (1,)), ((), ())), preferred_element_type=jnp.float32
            )
            top = None
            for part in range(plen // 32):
                for j in range(4):
                    at = part * 32 + j * 8
                    inside = 4 * sub + (part * 32 + j) < limit
                    tile = jnp.where(inside, scores[at : at + 8], MASKED)
                    top = tile if top is None else jnp.maximum(top, tile)
            line = jnp.max(top, axis=0, keepdims=True)
            for n in range(four):
                own = (lane_q[0:1] >= n * qtok) & (lane_q[0:1] < (n + 1) * qtok)
                totals[pl.ds(batch * BATCH + k * four + n, 1), :] = jnp.where(own, line, 0.0)
        return 0

    lax.fori_loop(0, 2 * srcs // BATCH, score_step, 0)

    value = jnp.sum(totals[...], axis=1, keepdims=True) * (1.0 / qtok)
    ends = ends_ref[...]
    lane = lax.broadcasted_iota(jnp.int32, (srcs, srcs), 1)
    place = jnp.right_shift(ends.astype(jnp.int32), pass_dev.bit_length() - 1)
    low, high = place[:, 0:1], place[:, 1:2]
    second = ends[:, 1:2] > ends[:, 0:1]
    part_ref[...] = jnp.where(lane == low, value[0:srcs], 0.0) + jnp.where(
        (lane == high) & second, value[srcs : 2 * srcs], 0.0
    )
    greeted()

    def rows_of(g):
        return part_ref.at[pl.ds(pl.multiple_of(g * cents, cents), cents)]

    blocks, tops, lines = [], [], []
    for d in range(1, groups):
        peer = lax.rem(me_g + d, groups)
        blocks.append(push(rows_of(peer), part_buf.at[me_g], s1.at[d], r1.at[d], "grp", peer))
    for d in range(1, cents):
        peer = lax.rem(me_c + d, cents)
        tops.append(push(best_ref, best_buf.at[me_c], sb.at[d], rb.at[d], "cent", peer))
        lines.append(push(sum_buf.at[peer], row_buf.at[me_c], s2.at[d], r2.at[d], "cent", peer))
    for copy in blocks:
        copy.start()
    for copy in tops:
        copy.start()
    part_buf[me_g] = part_ref[pl.ds(pl.multiple_of(me_g * cents, cents), cents), :]
    best_buf[me_c] = best_ref[...]
    for copy in blocks:
        copy.wait_recv()
    total = part_buf[0]
    for g in range(1, groups):
        total = total + part_buf[g]
    for c in range(cents):
        sum_buf[c] = total[c : c + 1, :]
    row_buf[me_c] = sum_buf[me_c]
    for copy in lines:
        copy.start()

    for copy in tops:
        copy.wait_recv()
    top = best_buf[0]
    for c in range(1, cents):
        top = jnp.maximum(top, best_buf[c])
    width = token_ref.shape[1]
    for r in range(token_ref.shape[0]):
        token_ref[r : r + 1, :] = top[:, r * width : (r + 1) * width]

    for copy in lines:
        copy.wait_recv()
    line = row_buf[0]
    for c in range(1, cents):
        line = line + row_buf[c]
    half = score_ref.shape[1]
    score_ref[0:1, :] = line[:, 0:half]
    score_ref[1:2, :] = line[:, half : 2 * half]
    for copy in blocks + tops + lines:
        copy.wait_send()


def shards(queries, centroids, candidates, token_codes, resid_words, lengths, levels):
    query_rows, qtok, width = queries.shape
    cent_dev = centroids.shape[0]
    pass_dev, plen = token_codes.shape
    packed = resid_words.shape[1]
    per_device, cand_count = candidates.shape[2:]
    cents, groups = lax.axis_size("cent"), lax.axis_size("grp")
    srcs = cents * groups
    tokens = query_rows * qtok
    block, head = 2048, cent_dev // 2
    tiles = tokens // 256
    mib = 1 << 20
    dma = pltpu.SemaphoreType.DMA
    f32, i32, bf16 = jnp.float32, jnp.int32, jnp.bfloat16
    sds = jax.ShapeDtypeStruct
    hbm = functools.partial(pltpu.with_memory_space_constraint, memory_space=pltpu.HBM)

    table, tail, words, qall, qt, acc, picks, ends, entries = pl.pallas_call(
        functools.partial(search_kernel, cents, groups, pass_dev, block, head, cand_count),
        out_shape=(
            sds((cent_dev, width), f32),
            sds((cent_dev - head, width), bf16),
            sds((pass_dev, packed, width), i32),
            sds((groups, tokens, width), bf16),
            sds((tiles, width, 256), bf16),
            sds((tiles, 8, 256), f32),
            sds((32, plen // 32 * pass_dev), i32),
            sds((srcs, srcs), f32),
            sds((8, srcs), i32),
        ),
        in_specs=[ANY] * 5,
        out_specs=(VMEM,) * 9,
        scratch_shapes=[
            pltpu.VMEM((per_device, cand_count), i32),
            pltpu.VMEM((pass_dev, plen), i32),
            pltpu.VMEM((head, width), bf16),
            pltpu.VMEM((cents, 1, srcs), i32),
            pltpu.VMEM((groups, cents, 1, srcs), i32),
            pltpu.VMEM((srcs, srcs), i32),
            dma((head // block,)),
            dma(((cent_dev - head) // block,)),
            dma,
            dma,
            dma,
            dma,
            dma((cents,)),
            dma((cents,)),
            dma((groups,)),
            dma((groups,)),
            dma((13,)),
            dma((13,)),
        ],
        compiler_params=pltpu.CompilerParams(
            collective_id=0, has_side_effects=True, vmem_limit_bytes=6 * mib
        ),
        name="search",
    )(
        hbm(queries.reshape(tokens, width)),
        hbm(candidates.reshape(per_device, cand_count)),
        hbm(token_codes),
        hbm(centroids),
        hbm(resid_words),
    )

    slots = 2 * srcs
    held = (slots + 1) * (plen // 32) + 2 * UNITS
    embeds, starts, best = pl.pallas_call(
        functools.partial(passage_kernel, cents, groups, pass_dev, plen, OPENING),
        out_shape=(sds((held, 32, width), bf16), sds((slots,), i32), sds((1, tokens), f32)),
        in_specs=[SMEM, SMEM] + [VMEM, ANY] + [VMEM] * 5,
        out_specs=(VMEM, SMEM, VMEM),
        scratch_shapes=[
            pltpu.SMEM((slots * (plen // 32) + UNITS + 4,), i32),
            pltpu.SMEM((pass_dev + 1,), i32),
            pltpu.VMEM((UNITS * 32, width), f32),
            pltpu.VMEM((tiles, 8, 256), f32),
            dma((32,)),
            *[pltpu.SMEM((plen // 32 * pass_dev,), i32) for _ in range(32)],
        ],
        compiler_params=pltpu.CompilerParams(vmem_limit_bytes=2 * mib),
        name="passages",
    )(entries.reshape(8 * srcs), lengths, levels, picks, table, tail, words, qt, acc)

    token_best, scores = pl.pallas_call(
        functools.partial(return_kernel, cents, groups, pass_dev, plen, qtok),
        out_shape=(sds((query_rows, qtok), f32), sds((per_device, cand_count), f32)),
        in_specs=[SMEM] * 3 + [VMEM] * 4,
        out_specs=(VMEM, VMEM),
        scratch_shapes=[
            pltpu.VMEM((srcs, srcs), f32),
            pltpu.VMEM((slots, 128), f32),
            [pltpu.VMEM((128, 128 // qtok * width), bf16) for _ in range(BATCH * qtok // 128)],
            pltpu.VMEM((cents, 1, tokens), f32),
            pltpu.VMEM((groups, cents, srcs), f32),
            pltpu.VMEM((cents, 1, srcs), f32),
            pltpu.VMEM((cents, 1, srcs), f32),
            dma((cents,)),
            dma((cents,)),
            dma((groups,)),
            dma((groups,)),
            dma((cents,)),
            dma((cents,)),
        ],
        compiler_params=pltpu.CompilerParams(
            collective_id=1, has_side_effects=True, vmem_limit_bytes=4 * mib
        ),
        name="returns",
    )(
        entries.reshape(8 * srcs),
        lengths,
        starts,
        ends,
        embeds,
        qall.reshape(groups * query_rows, qtok, width),
        best,
    )
    return token_best, scores.reshape(1, 1, per_device, cand_count)


def solution(mesh):
    placed = (
        P("grp", None, None),
        P("cent", None),
        P("grp", "cent", None, None),
        P(("cent", "grp"), None),
        P(("cent", "grp"), None, None),
        P(("cent", "grp")),
        P(),
    )
    return jax.shard_map(
        shards,
        mesh=mesh,
        in_specs=placed,
        out_specs=(P("grp", None), P("grp", "cent", None, None)),
        check_vma=False,
    )
```
